32 devices in a mesh: group: 4 (over z), seq: 8 (over y, x, core).
Axes of the slice: x: 2, y: 2, z: 4, core: 2. Of those that a mesh axis runs over, the one named last changes fastest.
Arguments:
- vis_query: bfloat16 [8, 32, 1280], P('group', 'seq'), parts along dimension 0, may hold values from -200 to 200
- vis_key: bfloat16 [8, 32, 1280], P('group', 'seq'), parts along dimension 0, may hold values from -200 to 200
- vis_value: bfloat16 [8, 32, 1280], P('group', 'seq'), parts along dimension 0, may hold values from -6 to 6
- vis_resid: bfloat16 [8, 32, 1280], P('group', 'seq'), parts along dimension 0, may hold values from -6 to 6
- attn_gate: float32 [1], replicated, may hold values from 0.3 to 1.5
- tile_count: int32 [8], P('group'), parts along dimension 0, may hold values from 1 to 4
- w_kv: bfloat16 [1280, 2048], replicated, may hold values from -0.15625 to 0.15625
- text_query: bfloat16 [4096, 6144], P(('group', 'seq')), parts along dimension 0, may hold values from -200 to 200
- text_image: int32 [4096], P(('group', 'seq')), parts along dimension 0, may hold values from 0 to 1, as said below
Outputs:
- vision_out: bfloat16 [8, 32, 1280], P('group', 'seq'), parts along dimension 0
- cross_out: bfloat16 [4096, 6144], P(('group', 'seq')), parts along dimension 0
The draws below stay inside these ranges and needn't reach their ends.
There are 4 independent parts, one for each index of `group`. The reference program is written for one: setup_inputs(seed, part) draws one part's arguments, and reference() takes and returns one part's arrays. A program takes and returns all parts, laid end to end along the dimension named above; an argument that names none is the same for every part. Nothing has to cross between parts.
Inputs may be any that keep to these rules, and one draw needn't show every extreme that they name: `text_image`: does not fall along the sequence; both values occur.
All inputs are finite; a program needn't handle non-finite values.
Results may differ from the reference program's by a relative error of at most 0.0035.
The reference program's roundings to bfloat16 on the way count: a program that leaves them out, or rounds other values in their place, can miss the bound.
Values may be sent and summed in bfloat16 or wider, within the bound.
A program may use at most 64 MiB of HBM per device.

```python
import math
import jax
import jax.numpy as jnp
from jax import lax

VHEADS = 16
KVH = 8
HD = 128
QGROUP = 6
IMAGES = 2
TILES = 4
VW = 1280
VIS = 32
TEXT = 1024


def vision_pair(key):
    first, second = jax.random.split(jax.random.fold_in(key, 11), 2)
    query = jax.random.normal(first, (IMAGES, VIS, VW), jnp.float32)
    keys = jax.random.normal(second, (IMAGES, VIS, VW), jnp.float32)
    query = jnp.clip(query, -6.0, 6.0)
    keys = jnp.clip(keys, -6.0, 6.0)
    return (query, keys)


def draw_vis_query(key, part):
    return vision_pair(key)[0].astype(jnp.bfloat16)


def draw_vis_key(key, part):
    return vision_pair(key)[1].astype(jnp.bfloat16)


def draw_text_query(key, part):
    first = jax.random.fold_in(jax.random.fold_in(key, 23), 0)
    values = jax.random.normal(first, (TEXT, KVH * QGROUP * HD), jnp.float32)
    values = jnp.clip(values, -6.0, 6.0)
    return values.astype(jnp.bfloat16)


def draw_text_image(key, part):
    border = jax.random.randint(jax.random.fold_in(key, 37), (), 1, TEXT)
    return (jnp.arange(TEXT, dtype=jnp.int32) >= border).astype(jnp.int32)


def levels(rng, shape, cuts, smallest, high):
    factor_of = 1.0
    for position, blocks in cuts:
        heights = jax.random.uniform(jax.random.fold_in(jax.random.fold_in(rng, 6), position), (blocks,), jnp.float32, smallest / len(cuts), high / len(cuts))
        factor_of = factor_of * jnp.repeat(jnp.exp(heights), shape[position] // blocks).reshape((-1,) + (1,) * (len(shape) - 1 - position))
    return factor_of


def gaussian(key, shape, spread, bound, cuts=(), held_as=jnp.bfloat16):
    factor_of = levels(key, shape, cuts, -0.22, 0.18) if cuts else 1.0
    entries = jax.random.normal(key, shape, jnp.float32) * spread * factor_of
    return jnp.minimum(jnp.maximum(entries, -bound), bound).astype(held_as)


def setup_inputs(seed: int = 0, part: int = 0) -> dict:
    splits = jax.random.split(jax.random.key(seed), 10)
    part_splits = jax.random.split(jax.random.fold_in(splits[9], part), 10)
    return {
        "vis_query": draw_vis_query(jax.random.fold_in(jax.random.fold_in(splits[9], part), 71), part),
        "vis_key": draw_vis_key(jax.random.fold_in(jax.random.fold_in(splits[9], part), 71), part),
        "vis_value": gaussian(part_splits[2], (IMAGES, VIS, VW), 1.0, 6.0, ((1, 8),)),
        "vis_resid": gaussian(part_splits[3], (IMAGES, VIS, VW), 1.0, 6.0, ((1, 8),)),
        "attn_gate": jnp.clip(jax.random.uniform(splits[4], (1,), jnp.float32, 0.3, 1.5), 0.3, 1.5),
        "tile_count": jax.random.randint(part_splits[5], (IMAGES,), 1, TILES + 1).astype(jnp.int32),
        "w_kv": gaussian(splits[6], (VW, 2 * KVH * HD), VW ** -0.5, 0.15625),
        "text_query": draw_text_query(jax.random.fold_in(jax.random.fold_in(splits[9], part), 71), part),
        "text_image": draw_text_image(jax.random.fold_in(jax.random.fold_in(splits[9], part), 71), part),
    }


def reference(vis_query, vis_key, vis_value, vis_resid, attn_gate, tile_count, w_kv, text_query, text_image):
    images, length, width = vis_query.shape
    hsize = width // VHEADS
    patch = length // TILES
    tile_of = jnp.arange(length, dtype=jnp.int32) // patch
    key_ok = tile_of[None, :] < tile_count[:, None]
    query = vis_query.astype(jnp.float32).reshape(images, length, VHEADS, hsize)
    keys = vis_key.astype(jnp.float32).reshape(images, length, VHEADS, hsize)
    values = vis_value.astype(jnp.float32).reshape(images, length, VHEADS, hsize)
    scores = jnp.einsum('bqhd,bkhd->bhqk', query, keys, precision=lax.Precision.HIGHEST) / math.sqrt(hsize)
    scores = jnp.where(key_ok[:, None, None, :], scores, -1e+30)
    peak = lax.optimization_barrier(jnp.max(scores, axis=-1, keepdims=True))
    expo = jnp.exp(scores - peak)
    probs = (expo / lax.optimization_barrier(jnp.sum(expo, axis=-1, keepdims=True))).astype(jnp.bfloat16)
    attn = jnp.einsum('bhqk,bkhd->bqhd', probs.astype(jnp.float32), values, precision=lax.Precision.HIGHEST)
    attn = attn.reshape(images, length, width)
    vision_out = (vis_resid.astype(jnp.float32) + jnp.tanh(attn_gate[0]) * attn).astype(jnp.bfloat16)
    cross_kv = jnp.dot(vision_out.reshape(images * length, width), w_kv, preferred_element_type=jnp.float32).astype(jnp.bfloat16)
    half = KVH * HD
    cross_key = cross_kv[:, :half].astype(jnp.float32).reshape(images * length, KVH, HD)
    cross_value = cross_kv[:, half:].astype(jnp.float32).reshape(images * length, KVH, HD)
    image_of_key = jnp.arange(images * length, dtype=jnp.int32) // length
    flat_ok = key_ok.reshape(images * length)
    total = text_query.shape[0]
    block = 512 if total % 512 == 0 else total
    count = total // block
    queries = text_query.reshape(count, block, KVH * QGROUP * HD)
    seen = text_image.reshape(count, block)

    def one_block(pair):
        rows, last = pair
        qrows = rows.astype(jnp.float32).reshape(block, KVH, QGROUP, HD)
        score = jnp.einsum('tgqd,kgd->tgqk', qrows, cross_key, precision=lax.Precision.HIGHEST) / math.sqrt(HD)
        allowed = (image_of_key[None, :] <= last[:, None]) & flat_ok[None, :]
        score = jnp.where(allowed[:, None, None, :], score, -1e+30)
        top = lax.optimization_barrier(jnp.max(score, axis=-1, keepdims=True))
        ex = jnp.exp(score - top)
        prob = (ex / lax.optimization_barrier(jnp.sum(ex, axis=-1, keepdims=True))).astype(jnp.bfloat16)
        out = jnp.einsum('tgqk,kgd->tgqd', prob.astype(jnp.float32), cross_value, precision=lax.Precision.HIGHEST)
        return out.reshape(block, KVH * QGROUP * HD).astype(jnp.bfloat16)
    cross_out = lax.map(one_block, (queries, seen)).reshape(total, KVH * QGROUP * HD)
    return (vision_out, cross_out)
```

```python
import functools
import math

import jax
import jax.numpy as jnp
from jax import lax
from jax.experimental import pallas as pl
from jax.experimental.pallas import tpu as pltpu
from jax.sharding import PartitionSpec as P

VHEADS = 16
VHEAD = 80
KVH = 8
HD = 128
QGROUP = 6
TILES = 4
LANES = 128
NEG = -1e30


def vision_attend(query, keys, values, tile_count, nheads):
    images, rows, width = query.shape
    length = keys.shape[1]
    patch = length // TILES
    tile_of = jnp.arange(length, dtype=jnp.int32) // patch
    key_ok = tile_of[None, :] < tile_count[:, None]
    query = query.reshape(images, rows, nheads, VHEAD)
    keys = keys.reshape(images, length, nheads, VHEAD)
    values = values.reshape(images, length, nheads, VHEAD)
    scores = jnp.einsum(
        "bqhd,bkhd->bhqk", query, keys, preferred_element_type=jnp.float32
    ) / math.sqrt(VHEAD)
    scores = jnp.where(key_ok[:, None, None, :], scores, NEG)
    peak = jnp.max(scores, axis=-1, keepdims=True)
    expo = jnp.exp(scores - peak)
    probs = (expo / jnp.sum(expo, axis=-1, keepdims=True)).astype(jnp.bfloat16)
    attn = jnp.einsum("bhqk,bkhd->bqhd", probs, values, preferred_element_type=jnp.float32)
    return attn.reshape(images, rows, width)


def general_form(
    vis_query, vis_key, vis_value, vis_resid, attn_gate, tile_count, w_kv, text_query, text_image
):
    images, rows, width = vis_query.shape
    keys, values = (
        lax.all_gather(vis_key, "seq", axis=1, tiled=True),
        lax.all_gather(vis_value, "seq", axis=1, tiled=True),
    )
    attn = vision_attend(vis_query, keys, values, tile_count, VHEADS)
    vision_out = (vis_resid.astype(jnp.float32) + jnp.tanh(attn_gate[0]) * attn).astype(
        jnp.bfloat16
    )
    local_kv = jnp.dot(
        vision_out.reshape(images * rows, width), w_kv, preferred_element_type=jnp.float32
    )
    local_kv = local_kv.astype(jnp.bfloat16).reshape(images, rows, w_kv.shape[1])
    cross_kv = lax.all_gather(local_kv, "seq", axis=1, tiled=True)
    length = cross_kv.shape[1]
    patch = length // TILES
    tile_of = jnp.arange(length, dtype=jnp.int32) // patch
    key_ok = tile_of[None, :] < tile_count[:, None]
    half = KVH * HD
    flat_kv = cross_kv.reshape(images * length, 2 * half)
    cross_key = flat_kv[:, :half].reshape(images * length, KVH, HD)
    cross_value = flat_kv[:, half:].reshape(images * length, KVH, HD)
    image_of_key = jnp.arange(images * length, dtype=jnp.int32) // length
    flat_ok = key_ok.reshape(images * length)
    tokens = text_query.shape[0]
    qrows = text_query.reshape(tokens, KVH, QGROUP, HD)
    score = jnp.einsum(
        "tgqd,kgd->tgqk", qrows, cross_key, preferred_element_type=jnp.float32
    ) / math.sqrt(HD)
    allowed = (image_of_key[None, :] <= text_image[:, None]) & flat_ok[None, :]
    score = jnp.where(allowed[:, None, None, :], score, NEG)
    top = jnp.max(score, axis=-1, keepdims=True)
    expd = jnp.exp(score - top)
    prob = (expd / jnp.sum(expd, axis=-1, keepdims=True)).astype(jnp.bfloat16)
    out = jnp.einsum("tgqk,kgd->tgqd", prob, cross_value, preferred_element_type=jnp.float32)
    cross_out = out.reshape(tokens, KVH * QGROUP * HD).astype(jnp.bfloat16)
    return (vision_out, cross_out)


GRANT = 16 * 1024 * 1024
MESH = pl.DeviceIdType.MESH
CORES = 2


def gather_kernel(
    n, images, rows, width, tokens,
    gate_in, count_in, seen_in, q_in, k_in, v_in, r_in, w_in, text_in,
    vis_ref, bias_ref, pick_ref, w_ref, text_ref,
    own, slots, seen_ref, gate_ref, count_ref,
    load_sem, mine_sem, small_sem, big_sem, send_sem, recv_sem, swap_sem,
):
    me = lax.axis_index("seq")
    chip, core = me // CORES, me % CORES
    row, col = chip // 2, chip % 2
    partner = chip * CORES + (1 - core)
    across = row * 2 + (1 - col)
    along = (1 - row) * 2 + col
    corner = (1 - row) * 2 + (1 - col)
    length = n * rows
    keys = images * length

    sources = (q_in, k_in, v_in, r_in)
    loads = [
        pltpu.make_async_copy(ref.at[b], own.at[b, a], load_sem.at[b, a])
        for b in range(images)
        for a, ref in enumerate(sources)
    ]
    loads += [
        pltpu.make_async_copy(ref.at[core], slots.at[me, a], mine_sem.at[a])
        for a, ref in enumerate(sources)
    ]
    barrier = pltpu.get_barrier_semaphore()
    chips = (corner, across, along)
    others = [there * CORES + b for there in chips for b in range(CORES)] + [partner]
    for dev in others:
        pl.semaphore_signal(barrier, inc=1, device_id={"seq": dev}, device_id_type=MESH)
    for load in loads:
        load.start()
    small = [
        pltpu.make_async_copy(gate_in, gate_ref, small_sem.at[0]),
        pltpu.make_async_copy(count_in, count_ref, small_sem.at[1]),
        pltpu.make_async_copy(seen_in, seen_ref, small_sem.at[2]),
    ]
    big = [
        pltpu.make_async_copy(w_in, w_ref, big_sem.at[0]),
        pltpu.make_async_copy(text_in, text_ref, big_sem.at[1]),
    ]
    for copy in small + big:
        copy.start()
    pl.semaphore_wait(barrier, len(others))
    for load in loads:
        load.wait()

    cuts = (pl.ds(0, 3), pl.ds(3, 1))

    def send(b, part, dev, number):
        return pltpu.make_async_remote_copy(
            src_ref=own.at[b, cuts[part]],
            dst_ref=slots.at[me, cuts[part]],
            send_sem=send_sem.at[part, number],
            recv_sem=recv_sem.at[me, part],
            device_id={"seq": dev},
            device_id_type=MESH,
        )

    sent = []
    for part in range(2):
        for number, there in enumerate(chips):
            for b in range(images):
                sent.append(send(b, part, there * CORES + b, number * CORES + b))
        sent.append(send(1 - core, part, partner, len(chips) * CORES))
    for copy in sent:
        copy.start()

    for copy in small:
        copy.wait()
    place = lax.broadcasted_iota(jnp.int32, (length, tokens), 0)
    for b in range(images):
        ok = (place // (length // TILES) < count_ref[b]) & (seen_ref[...] >= b)
        bias = jnp.where(ok, 0.0, NEG)
        for twin in range(2):
            at = twin * keys + b * length
            bias_ref[at : at + length, :] = bias
    line = lax.broadcasted_iota(jnp.int32, pick_ref.shape, 0)
    want = (line // 8) * length + me * rows + line % 8
    here = lax.broadcasted_iota(jnp.int32, pick_ref.shape, 1)
    pick_ref[...] = jnp.where(here == want, 1.0, 0.0).astype(jnp.bfloat16)
    gate = jnp.tanh(jnp.full((1, LANES), gate_ref[0], jnp.float32))

    def arrived(part):
        for dev in others:
            pltpu.make_async_remote_copy(
                src_ref=own.at[0, cuts[part]],
                dst_ref=slots.at[dev, cuts[part]],
                send_sem=send_sem.at[part, 0],
                recv_sem=recv_sem.at[dev, part],
                device_id={"seq": partner},
                device_id_type=MESH,
            ).wait_recv()

    def whole(a):
        return jnp.concatenate(
            [slots[s, a].astype(jnp.float32) for s in range(n)], axis=0
        )

    arrived(0)
    query, key, value = (whole(a).astype(jnp.bfloat16) for a in range(3))
    heads = width // VHEAD
    side = LANES // length
    groups = range(0, heads, side)
    key_row = lax.broadcasted_iota(jnp.int32, (length, LANES), 0)
    scale = math.log2(math.e) / math.sqrt(VHEAD)
    count = jnp.where(core == 0, count_ref[0], count_ref[1])
    bias = jnp.where(key_row // (length // TILES) < count, 0.0, NEG)
    windows, owners, scores = [], [], []
    for h in groups:
        lo, hi = h * VHEAD // LANES * LANES, -(-(h + side) * VHEAD // LANES) * LANES
        lane = lax.broadcasted_iota(jnp.int32, (length, hi - lo), 1) + lo
        masks = [(lane >= i * VHEAD) & (lane < (i + 1) * VHEAD) for i in range(h, h + side)]
        window = query[:, lo:hi]
        spread = jnp.concatenate(
            [jnp.where(mask, window, jnp.zeros_like(window)) for mask in masks], axis=0
        )
        score = lax.dot_general(
            key[:, lo:hi], spread, (((1,), (1,)), ((), ())),
            preferred_element_type=jnp.float32,
        )
        windows.append((lo, hi))
        owners.append(masks)
        scores.append(score + bias)
    probs = []
    for score in scores:
        expo = jnp.exp2((score - jnp.max(score, axis=0, keepdims=True)) * scale)
        prob = expo * (1.0 / jnp.sum(expo, axis=0, keepdims=True))
        probs.append(prob.astype(jnp.bfloat16))
    parts = [None] * (width // LANES)
    for (lo, hi), masks, prob in zip(windows, owners, probs):
        attn = lax.dot_general(
            prob, value[:, lo:hi], (((0,), (0,)), ((), ())),
            preferred_element_type=jnp.float32,
        )
        total = jnp.zeros((length, hi - lo), jnp.float32)
        for i, mask in enumerate(masks):
            total = jnp.where(mask, attn[i * length : (i + 1) * length], total)
        for t in range(lo // LANES, hi // LANES):
            piece = total[:, t * LANES - lo : (t + 1) * LANES - lo]
            parts[t] = piece if parts[t] is None else parts[t] + piece
    branch = jnp.concatenate(parts, axis=1) * jnp.tile(gate, (1, len(parts)))
    arrived(1)
    mine = pl.ds(pl.multiple_of(core * length, length), length)
    vis_ref[mine, :] = (whole(3) + branch).astype(jnp.bfloat16)

    def swap(at):
        return pltpu.make_async_remote_copy(
            src_ref=vis_ref.at[at],
            dst_ref=vis_ref.at[at],
            send_sem=swap_sem.at[0],
            recv_sem=swap_sem.at[1],
            device_id={"seq": partner},
            device_id_type=MESH,
        )

    swap(mine).start()
    for copy in sent:
        copy.wait_send()
    for copy in big:
        copy.wait()
    swap(mine).wait_send()
    swap(pl.ds(pl.multiple_of((1 - core) * length, length), length)).wait_recv()


def gather_part(n, q, k, v, r, gate, count, seen, w_kv, text):
    images, rows, width = q.shape
    length = n * rows
    keys = images * length
    tokens = seen.shape[0]
    hbm = pl.BlockSpec(memory_space=pltpu.HBM)
    vmem = pl.BlockSpec(memory_space=pltpu.VMEM)
    held = [
        pltpu.with_memory_space_constraint(x, pltpu.HBM)
        for x in (count, seen.reshape(1, tokens), q, k, v, r, w_kv, text)
    ]
    return pl.pallas_call(
        functools.partial(gather_kernel, n, images, rows, width, tokens),
        out_shape=(
            jax.ShapeDtypeStruct((keys, width), jnp.bfloat16),
            jax.ShapeDtypeStruct((2 * keys, tokens), jnp.float32),
            jax.ShapeDtypeStruct((8 * images, keys), jnp.bfloat16),
            jax.ShapeDtypeStruct(w_kv.shape, jnp.bfloat16),
            jax.ShapeDtypeStruct(text.shape, jnp.bfloat16),
        ),
        in_specs=[hbm] * 9,
        out_specs=(vmem,) * 5,
        scratch_shapes=[
            pltpu.VMEM((images, 4, rows, width), jnp.bfloat16),
            pltpu.VMEM((n, 4, rows, width), jnp.bfloat16),
            pltpu.VMEM((1, tokens), jnp.int32),
            pltpu.SMEM((1,), jnp.float32),
            pltpu.SMEM((images,), jnp.int32),
            pltpu.SemaphoreType.DMA((images, 4)),
            pltpu.SemaphoreType.DMA((4,)),
            pltpu.SemaphoreType.DMA((3,)),
            pltpu.SemaphoreType.DMA((2,)),
            pltpu.SemaphoreType.DMA((2, n - 1)),
            pltpu.SemaphoreType.DMA((n, 2)),
            pltpu.SemaphoreType.DMA((2,)),
        ],
        compiler_params=pltpu.CompilerParams(
            collective_id=0, has_side_effects=True, vmem_limit_bytes=GRANT
        ),
        name="vision",
    )(gate, *held)


def text_kernel(
    vis_ref, bias_ref, pick_ref, w_ref, q_ref,
    vis_out, out_hbm,
    local_ref, kv_ref, o_ref, local_sem, out_sem,
):
    images, rows, width = local_ref.shape
    keys = vis_ref.shape[0]
    vis = vis_ref[...]
    half = KVH * HD
    scale = math.log2(math.e) / math.sqrt(HD)
    span = QGROUP * HD
    copies = []

    def project(at):
        return jnp.dot(
            vis, w_ref[:, at : at + 2 * HD], preferred_element_type=jnp.float32
        ).astype(jnp.bfloat16)

    def double(x):
        zero = jnp.zeros_like(x)
        return jnp.concatenate(
            [jnp.concatenate([x, zero], axis=1), jnp.concatenate([zero, x], axis=1)], axis=0
        )

    def attend(g, k_two, v_two):
        for j in range(QGROUP // 2):
            cols = slice(g * span + 2 * j * HD, g * span + (2 * j + 2) * HD)
            score = lax.dot_general(
                k_two, q_ref[:, cols], (((1,), (1,)), ((), ())),
                preferred_element_type=jnp.float32,
            )
            score = score + bias_ref[...]
            probs = []
            for part in (score[:keys], score[keys:]):
                expd = jnp.exp2((part - jnp.max(part, axis=0, keepdims=True)) * scale)
                probs.append(expd * (1.0 / jnp.sum(expd, axis=0, keepdims=True)))
            prob = jnp.concatenate(probs, axis=0).astype(jnp.bfloat16)
            o_ref[:, cols] = lax.dot_general(
                prob, v_two, (((0,), (0,)), ((), ())), preferred_element_type=jnp.float32
            ).astype(jnp.bfloat16)
        cols = pl.ds(g * span, span)
        copies.append(
            pltpu.make_async_copy(o_ref.at[:, cols], out_hbm.at[:, cols], out_sem.at[g])
        )
        copies[-1].start()

    local = jnp.dot(pick_ref[...], vis, preferred_element_type=jnp.float32)
    for b in range(images):
        local_ref[b] = local[8 * b : 8 * b + rows].astype(jnp.bfloat16)
    copies.append(pltpu.make_async_copy(local_ref, vis_out, local_sem))
    copies[-1].start()
    for at in range(0, 2 * half, 2 * HD):
        kv_ref[:, at : at + 2 * HD] = project(at)
    for g in range(KVH):
        attend(
            g,
            double(kv_ref[:, g * HD : (g + 1) * HD]),
            double(kv_ref[:, half + g * HD : half + (g + 1) * HD]),
        )
    for copy in copies:
        copy.wait()


def text_part(shape, vis, bias, pick, w_kv, query):
    vmem = pl.BlockSpec(memory_space=pltpu.VMEM)
    anyspace = pl.BlockSpec(memory_space=pl.ANY)
    return pl.pallas_call(
        text_kernel,
        out_shape=(
            jax.ShapeDtypeStruct(shape, jnp.bfloat16),
            jax.ShapeDtypeStruct(query.shape, jnp.bfloat16),
        ),
        in_specs=[vmem] * 5,
        out_specs=(anyspace, anyspace),
        scratch_shapes=[
            pltpu.VMEM(shape, jnp.bfloat16),
            pltpu.VMEM((vis.shape[0], w_kv.shape[1]), jnp.bfloat16),
            pltpu.VMEM(query.shape, jnp.bfloat16),
            pltpu.SemaphoreType.DMA,
            pltpu.SemaphoreType.DMA((KVH,)),
        ],
        compiler_params=pltpu.CompilerParams(vmem_limit_bytes=GRANT),
        name="text",
    )(vis, bias, pick, w_kv, query)


def fits(n, images, rows, width):
    length = n * rows
    return (
        n == 4 * CORES
        and images == CORES
        and 2 * images * length == LANES
        and LANES % length == 0
        and (width // VHEAD) % (LANES // length) == 0
        and rows <= 8
        and length % 16 == 0
    )


def on_device(n, *args):
    vis_query, vis_key, vis_value, vis_resid, attn_gate, tile_count, w_kv, text_query, text_image = args
    images, rows, width = vis_query.shape
    if not fits(n, images, rows, width):
        return general_form(*args)
    held = gather_part(
        n, vis_query, vis_key, vis_value, vis_resid, attn_gate, tile_count, text_image,
        w_kv, text_query,
    )
    return text_part(vis_query.shape, *held)


def solution(mesh):
    placed = (
        P("group", "seq", None),
        P("group", "seq", None),
        P("group", "seq", None),
        P("group", "seq", None),
        P(),
        P("group"),
        P(),
        P(("group", "seq"), None),
        P(("group", "seq")),
    )
    return jax.shard_map(
        functools.partial(on_device, mesh.shape["seq"]),
        mesh=mesh,
        in_specs=placed,
        out_specs=(P("group", "seq", None), P(("group", "seq"), None)),
        check_vma=False,
    )
```

```python
import functools
import math

import jax
import jax.numpy as jnp
from jax import lax
from jax.experimental import pallas as pl
from jax.experimental.pallas import tpu as pltpu
from jax.sharding import PartitionSpec as P

VHEADS = 16
VHEAD = 80
KVH = 8
HD = 128
QGROUP = 6
TILES = 4
LANES = 128
NEG = -1e30


def vision_attend(query, keys, values, tile_count, nheads):
    images, rows, width = query.shape
    length = keys.shape[1]
    patch = length // TILES
    tile_of = jnp.arange(length, dtype=jnp.int32) // patch
    key_ok = tile_of[None, :] < tile_count[:, None]
    query = query.reshape(images, rows, nheads, VHEAD)
    keys = keys.reshape(images, length, nheads, VHEAD)
    values = values.reshape(images, length, nheads, VHEAD)
    scores = jnp.einsum(
        "bqhd,bkhd->bhqk", query, keys, preferred_element_type=jnp.float32
    ) / math.sqrt(VHEAD)
    scores = jnp.where(key_ok[:, None, None, :], scores, NEG)
    peak = jnp.max(scores, axis=-1, keepdims=True)
    expo = jnp.exp(scores - peak)
    probs = (expo / jnp.sum(expo, axis=-1, keepdims=True)).astype(jnp.bfloat16)
    attn = jnp.einsum("bhqk,bkhd->bqhd", probs, values, preferred_element_type=jnp.float32)
    return attn.reshape(images, rows, width)


def general_form(
    vis_query, vis_key, vis_value, vis_resid, attn_gate, tile_count, w_kv, text_query, text_image
):
    images, rows, width = vis_query.shape
    keys, values = (
        lax.all_gather(vis_key, "seq", axis=1, tiled=True),
        lax.all_gather(vis_value, "seq", axis=1, tiled=True),
    )
    attn = vision_attend(vis_query, keys, values, tile_count, VHEADS)
    vision_out = (vis_resid.astype(jnp.float32) + jnp.tanh(attn_gate[0]) * attn).astype(
        jnp.bfloat16
    )
    local_kv = jnp.dot(
        vision_out.reshape(images * rows, width), w_kv, preferred_element_type=jnp.float32
    )
    local_kv = local_kv.astype(jnp.bfloat16).reshape(images, rows, w_kv.shape[1])
    cross_kv = lax.all_gather(local_kv, "seq", axis=1, tiled=True)
    length = cross_kv.shape[1]
    patch = length // TILES
    tile_of = jnp.arange(length, dtype=jnp.int32) // patch
    key_ok = tile_of[None, :] < tile_count[:, None]
    half = KVH * HD
    flat_kv = cross_kv.reshape(images * length, 2 * half)
    cross_key = flat_kv[:, :half].reshape(images * length, KVH, HD)
    cross_value = flat_kv[:, half:].reshape(images * length, KVH, HD)
    image_of_key = jnp.arange(images * length, dtype=jnp.int32) // length
    flat_ok = key_ok.reshape(images * length)
    tokens = text_query.shape[0]
    qrows = text_query.reshape(tokens, KVH, QGROUP, HD)
    score = jnp.einsum(
        "tgqd,kgd->tgqk", qrows, cross_key, preferred_element_type=jnp.float32
    ) / math.sqrt(HD)
    allowed = (image_of_key[None, :] <= text_image[:, None]) & flat_ok[None, :]
    score = jnp.where(allowed[:, None, None, :], score, NEG)
    top = jnp.max(score, axis=-1, keepdims=True)
    expd = jnp.exp(score - top)
    prob = (expd / jnp.sum(expd, axis=-1, keepdims=True)).astype(jnp.bfloat16)
    out = jnp.einsum("tgqk,kgd->tgqd", prob, cross_value, preferred_element_type=jnp.float32)
    cross_out = out.reshape(tokens, KVH * QGROUP * HD).astype(jnp.bfloat16)
    return (vision_out, cross_out)


GRANT = 16 * 1024 * 1024
MESH = pl.DeviceIdType.MESH
CORES = 2


def gather_kernel(
    n, images, rows, width, tokens,
    gate_in, count_in, seen_in, q_in, k_in, v_in, r_in, w_in, text_in,
    vis_ref, bias_ref, pick_ref, w_ref, text_ref,
    other, slots, seen_ref, gate_ref, count_ref,
    load_sem, small_sem, big_sem, send_sem, recv_sem, swap_sem,
):
    me = lax.axis_index("seq")
    chip, core = me // CORES, me % CORES
    row, col = chip // 2, chip % 2
    partner = chip * CORES + (1 - core)
    across = row * 2 + (1 - col)
    along = (1 - row) * 2 + col
    corner = (1 - row) * 2 + (1 - col)
    length = n * rows
    keys = images * length

    sources = (q_in, k_in, v_in, r_in)
    mine = slots.at[me]
    loads = [
        pltpu.make_async_copy(ref.at[image], into.at[a], load_sem)
        for a, ref in enumerate(sources)
        for image, into in ((core, mine), (1 - core, other))
    ]

    def all_of(ref, sem):
        return pltpu.make_async_copy(ref, ref, sem)

    barrier = pltpu.get_barrier_semaphore()
    chips = (corner, across, along)
    others = [there * CORES + b for there in chips for b in range(CORES)] + [partner]
    for dev in others:
        pl.semaphore_signal(barrier, inc=1, device_id={"seq": dev}, device_id_type=MESH)
    for load in loads:
        load.start()
    small = [
        pltpu.make_async_copy(gate_in, gate_ref, small_sem.at[0]),
        pltpu.make_async_copy(count_in, count_ref, small_sem.at[1]),
        pltpu.make_async_copy(seen_in, seen_ref, small_sem.at[2]),
    ]
    big = [
        pltpu.make_async_copy(w_in, w_ref, big_sem.at[0]),
        pltpu.make_async_copy(text_in, text_ref, big_sem.at[1]),
    ]
    for copy in small:
        copy.start()
    pl.semaphore_wait(barrier, len(others))
    all_of(slots.at[:2], load_sem).wait()

    cuts = (pl.ds(0, 3), pl.ds(3, 1))

    def send(src, part, dev):
        pltpu.make_async_remote_copy(
            src_ref=src.at[cuts[part]],
            dst_ref=slots.at[me, cuts[part]],
            send_sem=send_sem,
            recv_sem=recv_sem.at[part],
            device_id={"seq": dev},
            device_id_type=MESH,
        ).start()

    for part in range(2):
        for there in chips:
            send(mine, part, there * CORES + core)
            send(other, part, there * CORES + 1 - core)
        send(other, part, partner)
    for copy in big:
        copy.start()

    for copy in small:
        copy.wait()
    place = lax.broadcasted_iota(jnp.int32, (length, tokens), 0)
    for b in range(images):
        ok = (place // (length // TILES) < count_ref[b]) & (seen_ref[...] >= b)
        bias = jnp.where(ok, 0.0, NEG)
        for twin in range(2):
            at = twin * keys + b * length
            bias_ref[at : at + length, :] = bias
    line = lax.broadcasted_iota(jnp.int32, pick_ref.shape, 0)
    want = (line // 8) * length + me * rows + line % 8
    key_at = lax.broadcasted_iota(jnp.int32, pick_ref.shape, 1)
    pick_ref[...] = jnp.where(key_at == want, 1.0, 0.0).astype(jnp.bfloat16)
    gate = jnp.tanh(jnp.full((1, LANES), gate_ref[0], jnp.float32))

    def arrived(part):
        all_of(slots.at[: n - 1, cuts[part]], recv_sem.at[part]).wait()

    def whole(a):
        return jnp.concatenate(
            [slots[s, a].astype(jnp.float32) for s in range(n)], axis=0
        )

    arrived(0)
    query, key, value = (whole(a).astype(jnp.bfloat16) for a in range(3))
    heads = width // VHEAD
    side = LANES // length
    groups = range(0, heads, side)
    key_row = lax.broadcasted_iota(jnp.int32, (length, LANES), 0)
    scale = math.log2(math.e) / math.sqrt(VHEAD)
    count = jnp.where(core == 0, count_ref[0], count_ref[1])
    bias = jnp.where(key_row // (length // TILES) < count, 0.0, NEG)
    windows, owners, scores = [], [], []
    for h in groups:
        lo, hi = h * VHEAD // LANES * LANES, -(-(h + side) * VHEAD // LANES) * LANES
        lane = lax.broadcasted_iota(jnp.int32, (length, hi - lo), 1) + lo
        masks = [(lane >= i * VHEAD) & (lane < (i + 1) * VHEAD) for i in range(h, h + side)]
        window = query[:, lo:hi]
        spread = jnp.concatenate(
            [jnp.where(mask, window, jnp.zeros_like(window)) for mask in masks], axis=0
        )
        score = lax.dot_general(
            key[:, lo:hi], spread, (((1,), (1,)), ((), ())),
            preferred_element_type=jnp.float32,
        )
        windows.append((lo, hi))
        owners.append(masks)
        scores.append(score + bias)
    probs = []
    for score in scores:
        expo = jnp.exp2((score - jnp.max(score, axis=0, keepdims=True)) * scale)
        prob = expo * (1.0 / jnp.sum(expo, axis=0, keepdims=True))
        probs.append(prob.astype(jnp.bfloat16))
    parts = [None] * (width // LANES)
    for (lo, hi), masks, prob in zip(windows, owners, probs):
        attn = lax.dot_general(
            prob, value[:, lo:hi], (((0,), (0,)), ((), ())),
            preferred_element_type=jnp.float32,
        )
        total = jnp.zeros((length, hi - lo), jnp.float32)
        for i, mask in enumerate(masks):
            total = jnp.where(mask, attn[i * length : (i + 1) * length], total)
        for t in range(lo // LANES, hi // LANES):
            piece = total[:, t * LANES - lo : (t + 1) * LANES - lo]
            parts[t] = piece if parts[t] is None else parts[t] + piece
    branch = jnp.concatenate(parts, axis=1) * jnp.tile(gate, (1, len(parts)))
    arrived(1)
    here = pl.ds(pl.multiple_of(core * length, length), length)
    vis_ref[here, :] = (whole(3) + branch).astype(jnp.bfloat16)

    def swap(at):
        return pltpu.make_async_remote_copy(
            src_ref=vis_ref.at[at],
            dst_ref=vis_ref.at[at],
            send_sem=swap_sem.at[0],
            recv_sem=swap_sem.at[1],
            device_id={"seq": partner},
            device_id_type=MESH,
        )

    swap(here).start()
    all_of(slots.at[: n - 1], send_sem).wait()
    for copy in big:
        copy.wait()
    swap(here).wait_send()
    swap(pl.ds(pl.multiple_of((1 - core) * length, length), length)).wait_recv()


def gather_part(n, q, k, v, r, gate, count, seen, w_kv, text):
    images, rows, width = q.shape
    length = n * rows
    keys = images * length
    tokens = seen.shape[0]
    hbm = pl.BlockSpec(memory_space=pltpu.HBM)
    vmem = pl.BlockSpec(memory_space=pltpu.VMEM)
    held = [
        pltpu.with_memory_space_constraint(x, pltpu.HBM)
        for x in (count, seen.reshape(1, tokens), q, k, v, r, w_kv, text)
    ]
    return pl.pallas_call(
        functools.partial(gather_kernel, n, images, rows, width, tokens),
        out_shape=(
            jax.ShapeDtypeStruct((keys, width), jnp.bfloat16),
            jax.ShapeDtypeStruct((2 * keys, tokens), jnp.float32),
            jax.ShapeDtypeStruct((8 * images, keys), jnp.bfloat16),
            jax.ShapeDtypeStruct(w_kv.shape, jnp.bfloat16),
            jax.ShapeDtypeStruct(text.shape, jnp.bfloat16),
        ),
        in_specs=[hbm] * 9,
        out_specs=(vmem,) * 5,
        scratch_shapes=[
            pltpu.VMEM((4, rows, width), jnp.bfloat16),
            pltpu.VMEM((n, 4, rows, width), jnp.bfloat16),
            pltpu.VMEM((1, tokens), jnp.int32),
            pltpu.SMEM((1,), jnp.float32),
            pltpu.SMEM((images,), jnp.int32),
            pltpu.SemaphoreType.DMA,
            pltpu.SemaphoreType.DMA((3,)),
            pltpu.SemaphoreType.DMA((2,)),
            pltpu.SemaphoreType.DMA,
            pltpu.SemaphoreType.DMA((2,)),
            pltpu.SemaphoreType.DMA((2,)),
        ],
        compiler_params=pltpu.CompilerParams(
            collective_id=0, has_side_effects=True, vmem_limit_bytes=GRANT
        ),
        name="vision",
    )(gate, *held)


def text_kernel(
    vis_ref, bias_ref, pick_ref, w_ref, q_ref,
    vis_out, out_hbm,
    local_ref, kv_ref, o_ref, local_sem, out_sem,
):
    images, rows, width = local_ref.shape
    keys = vis_ref.shape[0]
    vis = vis_ref[...]
    half = KVH * HD
    scale = math.log2(math.e) / math.sqrt(HD)
    span = QGROUP * HD
    copies = []

    def project(at):
        return jnp.dot(
            vis, w_ref[:, at : at + 2 * HD], preferred_element_type=jnp.float32
        ).astype(jnp.bfloat16)

    def double(x):
        zero = jnp.zeros_like(x)
        return jnp.concatenate(
            [jnp.concatenate([x, zero], axis=1), jnp.concatenate([zero, x], axis=1)], axis=0
        )

    def attend(g, k_two, v_two):
        for j in range(QGROUP // 2):
            cols = slice(g * span + 2 * j * HD, g * span + (2 * j + 2) * HD)
            score = lax.dot_general(
                k_two, q_ref[:, cols], (((1,), (1,)), ((), ())),
                preferred_element_type=jnp.float32,
            )
            score = score + bias_ref[...]
            probs = []
            for part in (score[:keys], score[keys:]):
                expd = jnp.exp2((part - jnp.max(part, axis=0, keepdims=True)) * scale)
                probs.append(expd * (1.0 / jnp.sum(expd, axis=0, keepdims=True)))
            prob = jnp.concatenate(probs, axis=0).astype(jnp.bfloat16)
            o_ref[:, cols] = lax.dot_general(
                prob, v_two, (((0,), (0,)), ((), ())), preferred_element_type=jnp.float32
            ).astype(jnp.bfloat16)
        cols = pl.ds(g * span, span)
        copies.append(
            pltpu.make_async_copy(o_ref.at[:, cols], out_hbm.at[:, cols], out_sem.at[g])
        )
        copies[-1].start()

    local = jnp.dot(pick_ref[...], vis, preferred_element_type=jnp.float32)
    for b in range(images):
        local_ref[b] = local[8 * b : 8 * b + rows].astype(jnp.bfloat16)
    copies.append(pltpu.make_async_copy(local_ref, vis_out, local_sem))
    copies[-1].start()
    for at in range(0, 2 * half, 2 * HD):
        kv_ref[:, at : at + 2 * HD] = project(at)
    for g in range(KVH):
        attend(
            g,
            double(kv_ref[:, g * HD : (g + 1) * HD]),
            double(kv_ref[:, half + g * HD : half + (g + 1) * HD]),
        )
    for copy in copies:
        copy.wait()


def text_part(shape, vis, bias, pick, w_kv, query):
    vmem = pl.BlockSpec(memory_space=pltpu.VMEM)
    anyspace = pl.BlockSpec(memory_space=pl.ANY)
    return pl.pallas_call(
        text_kernel,
        out_shape=(
            jax.ShapeDtypeStruct(shape, jnp.bfloat16),
            jax.ShapeDtypeStruct(query.shape, jnp.bfloat16),
        ),
        in_specs=[vmem] * 5,
        out_specs=(anyspace, anyspace),
        scratch_shapes=[
            pltpu.VMEM(shape, jnp.bfloat16),
            pltpu.VMEM((vis.shape[0], w_kv.shape[1]), jnp.bfloat16),
            pltpu.VMEM(query.shape, jnp.bfloat16),
            pltpu.SemaphoreType.DMA,
            pltpu.SemaphoreType.DMA((KVH,)),
        ],
        compiler_params=pltpu.CompilerParams(vmem_limit_bytes=GRANT),
        name="text",
    )(vis, bias, pick, w_kv, query)


def fits(n, images, rows, width):
    length = n * rows
    return (
        n == 4 * CORES
        and images == CORES
        and 2 * images * length == LANES
        and LANES % length == 0
        and (width // VHEAD) % (LANES // length) == 0
        and rows <= 8
        and length % 16 == 0
    )


def on_device(n, *args):
    vis_query, vis_key, vis_value, vis_resid, attn_gate, tile_count, w_kv, text_query, text_image = args
    images, rows, width = vis_query.shape
    if not fits(n, images, rows, width):
        return general_form(*args)
    held = gather_part(
        n, vis_query, vis_key, vis_value, vis_resid, attn_gate, tile_count, text_image,
        w_kv, text_query,
    )
    return text_part(vis_query.shape, *held)


def solution(mesh):
    placed = (
        P("group", "seq", None),
        P("group", "seq", None),
        P("group", "seq", None),
        P("group", "seq", None),
        P(),
        P("group"),
        P(),
        P(("group", "seq"), None),
        P(("group", "seq")),
    )
    return jax.shard_map(
        functools.partial(on_device, mesh.shape["seq"]),
        mesh=mesh,
        in_specs=placed,
        out_specs=(P("group", "seq", None), P(("group", "seq"), None)),
        check_vma=False,
    )
```

```python
import functools
import math

import jax
import jax.numpy as jnp
from jax import lax
from jax.experimental import pallas as pl
from jax.experimental.pallas import tpu as pltpu
from jax.sharding import PartitionSpec as P

VHEADS = 16
VHEAD = 80
KVH = 8
HD = 128
QGROUP = 6
TILES = 4
LANES = 128
NEG = -1e30


def vision_attend(query, keys, values, tile_count, nheads):
    images, rows, width = query.shape
    length = keys.shape[1]
    patch = length // TILES
    tile_of = jnp.arange(length, dtype=jnp.int32) // patch
    key_ok = tile_of[None, :] < tile_count[:, None]
    query = query.reshape(images, rows, nheads, VHEAD)
    keys = keys.reshape(images, length, nheads, VHEAD)
    values = values.reshape(images, length, nheads, VHEAD)
    scores = jnp.einsum(
        "bqhd,bkhd->bhqk", query, keys, preferred_element_type=jnp.float32
    ) / math.sqrt(VHEAD)
    scores = jnp.where(key_ok[:, None, None, :], scores, NEG)
    peak = jnp.max(scores, axis=-1, keepdims=True)
    expo = jnp.exp(scores - peak)
    probs = (expo / jnp.sum(expo, axis=-1, keepdims=True)).astype(jnp.bfloat16)
    attn = jnp.einsum("bhqk,bkhd->bqhd", probs, values, preferred_element_type=jnp.float32)
    return attn.reshape(images, rows, width)


def general_form(
    vis_query, vis_key, vis_value, vis_resid, attn_gate, tile_count, w_kv, text_query, text_image
):
    images, rows, width = vis_query.shape
    keys, values = (
        lax.all_gather(vis_key, "seq", axis=1, tiled=True),
        lax.all_gather(vis_value, "seq", axis=1, tiled=True),
    )
    attn = vision_attend(vis_query, keys, values, tile_count, VHEADS)
    vision_out = (vis_resid.astype(jnp.float32) + jnp.tanh(attn_gate[0]) * attn).astype(
        jnp.bfloat16
    )
    local_kv = jnp.dot(
        vision_out.reshape(images * rows, width), w_kv, preferred_element_type=jnp.float32
    )
    local_kv = local_kv.astype(jnp.bfloat16).reshape(images, rows, w_kv.shape[1])
    cross_kv = lax.all_gather(local_kv, "seq", axis=1, tiled=True)
    length = cross_kv.shape[1]
    patch = length // TILES
    tile_of = jnp.arange(length, dtype=jnp.int32) // patch
    key_ok = tile_of[None, :] < tile_count[:, None]
    half = KVH * HD
    flat_kv = cross_kv.reshape(images * length, 2 * half)
    cross_key = flat_kv[:, :half].reshape(images * length, KVH, HD)
    cross_value = flat_kv[:, half:].reshape(images * length, KVH, HD)
    image_of_key = jnp.arange(images * length, dtype=jnp.int32) // length
    flat_ok = key_ok.reshape(images * length)
    tokens = text_query.shape[0]
    qrows = text_query.reshape(tokens, KVH, QGROUP, HD)
    score = jnp.einsum(
        "tgqd,kgd->tgqk", qrows, cross_key, preferred_element_type=jnp.float32
    ) / math.sqrt(HD)
    allowed = (image_of_key[None, :] <= text_image[:, None]) & flat_ok[None, :]
    score = jnp.where(allowed[:, None, None, :], score, NEG)
    top = jnp.max(score, axis=-1, keepdims=True)
    expd = jnp.exp(score - top)
    prob = (expd / jnp.sum(expd, axis=-1, keepdims=True)).astype(jnp.bfloat16)
    out = jnp.einsum("tgqk,kgd->tgqd", prob, cross_value, preferred_element_type=jnp.float32)
    cross_out = out.reshape(tokens, KVH * QGROUP * HD).astype(jnp.bfloat16)
    return (vision_out, cross_out)


GRANT = 16 * 1024 * 1024
MESH = pl.DeviceIdType.MESH
CORES = 2


def gather_kernel(
    n, images, rows, width, tokens,
    gate_in, count_in, seen_in, q_in, k_in, v_in, r_in, w_in, text_in,
    vis_ref, bias_ref, pick_ref, w_ref, text_ref,
    other, slots, seen_ref, gate_ref, count_ref,
    load_sem, small_sem, big_sem, send_sem, recv_sem, swap_sem,
):
    me = lax.axis_index("seq")
    chip, core = me // CORES, me % CORES
    row, col = chip // 2, chip % 2
    partner = chip * CORES + (1 - core)
    across = row * 2 + (1 - col)
    along = (1 - row) * 2 + col
    corner = (1 - row) * 2 + (1 - col)
    length = n * rows
    keys = images * length

    sources = (q_in, k_in, v_in, r_in)
    mine = slots.at[me]
    loads = [
        pltpu.make_async_copy(ref.at[image], into.at[a], load_sem)
        for a, ref in enumerate(sources)
        for image, into in ((core, mine), (1 - core, other))
    ]

    def all_of(ref, sem):
        return pltpu.make_async_copy(ref, ref, sem)

    barrier = pltpu.get_barrier_semaphore()
    chips = (corner, across, along)
    others = [there * CORES + b for there in chips for b in range(CORES)] + [partner]
    for dev in others:
        pl.semaphore_signal(barrier, inc=1, device_id={"seq": dev}, device_id_type=MESH)
    for load in loads:
        load.start()
    small = [
        pltpu.make_async_copy(gate_in, gate_ref, small_sem.at[0]),
        pltpu.make_async_copy(count_in, count_ref, small_sem.at[1]),
        pltpu.make_async_copy(seen_in, seen_ref, small_sem.at[2]),
    ]
    big = [
        pltpu.make_async_copy(w_in, w_ref, big_sem.at[0]),
        pltpu.make_async_copy(text_in, text_ref, big_sem.at[1]),
    ]
    for copy in small:
        copy.start()
    pl.semaphore_wait(barrier, len(others))
    all_of(slots.at[:2], load_sem).wait()

    cuts = (pl.ds(0, 3), pl.ds(3, 1))

    def send(src, part, dev):
        pltpu.make_async_remote_copy(
            src_ref=src.at[cuts[part]],
            dst_ref=slots.at[me, cuts[part]],
            send_sem=send_sem,
            recv_sem=recv_sem.at[part],
            device_id={"seq": dev},
            device_id_type=MESH,
        ).start()

    for part in range(2):
        for there in chips:
            send(mine, part, there * CORES + core)
            send(other, part, there * CORES + 1 - core)
        send(other, part, partner)
    for copy in big:
        copy.start()

    for copy in small:
        copy.wait()
    place = lax.broadcasted_iota(jnp.int32, (length, tokens), 0)
    for b in range(images):
        ok = (place // (length // TILES) < count_ref[b]) & (seen_ref[...] >= b)
        bias = jnp.where(ok, 0.0, NEG)
        for twin in range(2):
            at = twin * keys + b * length
            bias_ref[at : at + length, :] = bias
    line = lax.broadcasted_iota(jnp.int32, pick_ref.shape, 0)
    want = (line // 8) * length + me * rows + line % 8
    key_at = lax.broadcasted_iota(jnp.int32, pick_ref.shape, 1)
    pick_ref[...] = jnp.where(key_at == want, 1.0, 0.0).astype(jnp.bfloat16)
    gate = jnp.tanh(jnp.full((1, LANES), gate_ref[0], jnp.float32))

    def arrived(part):
        all_of(slots.at[: n - 1, cuts[part]], recv_sem.at[part]).wait()

    def whole(a):
        return jnp.concatenate(
            [slots[s, a].astype(jnp.float32) for s in range(n)], axis=0
        )

    arrived(0)
    query, key, value = (whole(a).astype(jnp.bfloat16) for a in range(3))
    heads = width // VHEAD
    side = LANES // length
    groups = range(0, heads, side)
    key_row = lax.broadcasted_iota(jnp.int32, (length, LANES), 0)
    scale = math.log2(math.e) / math.sqrt(VHEAD)
    count = jnp.where(core == 0, count_ref[0], count_ref[1])
    bias = jnp.where(key_row // (length // TILES) < count, 0.0, NEG)
    windows, owners, scores = [], [], []
    for h in groups:
        lo, hi = h * VHEAD // LANES * LANES, -(-(h + side) * VHEAD // LANES) * LANES
        lane = lax.broadcasted_iota(jnp.int32, (length, hi - lo), 1) + lo
        masks = [(lane >= i * VHEAD) & (lane < (i + 1) * VHEAD) for i in range(h, h + side)]
        window = query[:, lo:hi]
        spread = jnp.concatenate(
            [jnp.where(mask, window, jnp.zeros_like(window)) for mask in masks], axis=0
        )
        score = lax.dot_general(
            key[:, lo:hi], spread, (((1,), (1,)), ((), ())),
            preferred_element_type=jnp.float32,
        )
        windows.append((lo, hi))
        owners.append(masks)
        scores.append(score + bias)
    probs = []
    for score in scores:
        expo = jnp.exp2((score - jnp.max(score, axis=0, keepdims=True)) * scale)
        prob = expo * (1.0 / jnp.sum(expo, axis=0, keepdims=True))
        probs.append(prob.astype(jnp.bfloat16))
    parts = [None] * (width // LANES)
    for (lo, hi), masks, prob in zip(windows, owners, probs):
        attn = lax.dot_general(
            prob, value[:, lo:hi], (((0,), (0,)), ((), ())),
            preferred_element_type=jnp.float32,
        )
        total = jnp.zeros((length, hi - lo), jnp.float32)
        for i, mask in enumerate(masks):
            total = jnp.where(mask, attn[i * length : (i + 1) * length], total)
        for t in range(lo // LANES, hi // LANES):
            piece = total[:, t * LANES - lo : (t + 1) * LANES - lo]
            parts[t] = piece if parts[t] is None else parts[t] + piece
    branch = jnp.concatenate(parts, axis=1) * jnp.tile(gate, (1, len(parts)))
    arrived(1)
    here = pl.ds(pl.multiple_of(core * length, length), length)
    vis_ref[here, :] = (whole(3) + branch).astype(jnp.bfloat16)

    def swap(at):
        return pltpu.make_async_remote_copy(
            src_ref=vis_ref.at[at],
            dst_ref=vis_ref.at[at],
            send_sem=swap_sem.at[0],
            recv_sem=swap_sem.at[1],
            device_id={"seq": partner},
            device_id_type=MESH,
        )

    swap(here).start()
    all_of(slots.at[: n - 1], send_sem).wait()
    for copy in big:
        copy.wait()
    swap(here).wait_send()
    swap(pl.ds(pl.multiple_of((1 - core) * length, length), length)).wait_recv()


def gather_part(n, q, k, v, r, gate, count, seen, w_kv, text):
    images, rows, width = q.shape
    length = n * rows
    keys = images * length
    tokens = seen.shape[0]
    hbm = pl.BlockSpec(memory_space=pltpu.HBM)
    vmem = pl.BlockSpec(memory_space=pltpu.VMEM)
    held = [
        pltpu.with_memory_space_constraint(x, pltpu.HBM)
        for x in (count, seen.reshape(1, tokens), q, k, v, r, w_kv, text)
    ]
    return pl.pallas_call(
        functools.partial(gather_kernel, n, images, rows, width, tokens),
        out_shape=(
            jax.ShapeDtypeStruct((keys, width), jnp.bfloat16),
            jax.ShapeDtypeStruct((2 * keys, tokens), jnp.float32),
            jax.ShapeDtypeStruct((8 * images, keys), jnp.bfloat16),
            jax.ShapeDtypeStruct(w_kv.shape, jnp.bfloat16),
            jax.ShapeDtypeStruct(text.shape, jnp.bfloat16),
        ),
        in_specs=[hbm] * 9,
        out_specs=(vmem,) * 5,
        scratch_shapes=[
            pltpu.VMEM((4, rows, width), jnp.bfloat16),
            pltpu.VMEM((n, 4, rows, width), jnp.bfloat16),
            pltpu.VMEM((1, tokens), jnp.int32),
            pltpu.SMEM((1,), jnp.float32),
            pltpu.SMEM((images,), jnp.int32),
            pltpu.SemaphoreType.DMA,
            pltpu.SemaphoreType.DMA((3,)),
            pltpu.SemaphoreType.DMA((2,)),
            pltpu.SemaphoreType.DMA,
            pltpu.SemaphoreType.DMA((2,)),
            pltpu.SemaphoreType.DMA((2,)),
        ],
        compiler_params=pltpu.CompilerParams(
            collective_id=0, has_side_effects=True, vmem_limit_bytes=GRANT
        ),
        name="vision",
    )(gate, *held)


def text_kernel(
    vis_ref, bias_ref, pick_ref, w_ref, q_ref,
    vis_out, out_hbm,
    local_ref, kv_ref, o_ref, local_sem, out_sem,
):
    images, rows, width = local_ref.shape
    keys = vis_ref.shape[0]
    vis = vis_ref[...]
    half = KVH * HD
    scale = math.log2(math.e) / math.sqrt(HD)
    span = QGROUP * HD

    def project(at):
        return jnp.dot(
            vis, w_ref[:, at : at + 2 * HD], preferred_element_type=jnp.float32
        ).astype(jnp.bfloat16)

    def double(x):
        zero = jnp.zeros_like(x)
        return jnp.concatenate(
            [jnp.concatenate([x, zero], axis=1), jnp.concatenate([zero, x], axis=1)], axis=0
        )

    def attend(g, k_two, v_two):
        pairs = QGROUP // 2
        wide = 2 * HD
        scores = [
            lax.dot_general(
                k_two, q_ref[:, g * span + j * wide : g * span + (j + 1) * wide],
                (((1,), (1,)), ((), ())), preferred_element_type=jnp.float32,
            )
            for j in range(pairs)
        ]
        bias = bias_ref[:keys, :]
        probs = []
        for score in scores:
            halves = []
            for part in (score[:keys], score[keys:]):
                part = part + bias
                expd = jnp.exp2((part - jnp.max(part, axis=0, keepdims=True)) * scale)
                halves.append(expd * (1.0 / jnp.sum(expd, axis=0, keepdims=True)))
            probs.append(jnp.concatenate(halves, axis=0).astype(jnp.bfloat16))
        out = lax.dot_general(
            jnp.concatenate(probs, axis=1), v_two, (((0,), (0,)), ((), ())),
            preferred_element_type=jnp.float32,
        ).astype(jnp.bfloat16)
        tokens = out.shape[0] // pairs
        for j in range(pairs):
            o_ref[:, g * span + j * wide : g * span + (j + 1) * wide] = out[
                j * tokens : (j + 1) * tokens
            ]
        cols = pl.ds(g * span, span)
        pltpu.make_async_copy(o_ref.at[:, cols], out_hbm.at[:, cols], out_sem).start()

    local = jnp.dot(pick_ref[...], vis, preferred_element_type=jnp.float32)
    for b in range(images):
        local_ref[b] = local[8 * b : 8 * b + rows].astype(jnp.bfloat16)
    local_copy = pltpu.make_async_copy(local_ref, vis_out, local_sem)
    local_copy.start()
    for at in range(0, 2 * half, 2 * HD):
        kv_ref[:, at : at + 2 * HD] = project(at)
    for g in range(KVH):
        attend(
            g,
            double(kv_ref[:, g * HD : (g + 1) * HD]),
            double(kv_ref[:, half + g * HD : half + (g + 1) * HD]),
        )
    local_copy.wait()
    pltpu.make_async_copy(o_ref, out_hbm, out_sem).wait()


def text_part(shape, vis, bias, pick, w_kv, query):
    vmem = pl.BlockSpec(memory_space=pltpu.VMEM)
    anyspace = pl.BlockSpec(memory_space=pl.ANY)
    return pl.pallas_call(
        text_kernel,
        out_shape=(
            jax.ShapeDtypeStruct(shape, jnp.bfloat16),
            jax.ShapeDtypeStruct(query.shape, jnp.bfloat16),
        ),
        in_specs=[vmem] * 5,
        out_specs=(anyspace, anyspace),
        scratch_shapes=[
            pltpu.VMEM(shape, jnp.bfloat16),
            pltpu.VMEM((vis.shape[0], w_kv.shape[1]), jnp.bfloat16),
            pltpu.VMEM(query.shape, jnp.bfloat16),
            pltpu.SemaphoreType.DMA,
            pltpu.SemaphoreType.DMA,
        ],
        compiler_params=pltpu.CompilerParams(vmem_limit_bytes=GRANT),
        name="text",
    )(vis, bias, pick, w_kv, query)


def fits(n, images, rows, width):
    length = n * rows
    return (
        n == 4 * CORES
        and images == CORES
        and 2 * images * length == LANES
        and LANES % length == 0
        and (width // VHEAD) % (LANES // length) == 0
        and rows <= 8
        and length % 16 == 0
    )


def on_device(n, *args):
    vis_query, vis_key, vis_value, vis_resid, attn_gate, tile_count, w_kv, text_query, text_image = args
    images, rows, width = vis_query.shape
    if not fits(n, images, rows, width):
        return general_form(*args)
    held = gather_part(
        n, vis_query, vis_key, vis_value, vis_resid, attn_gate, tile_count, text_image,
        w_kv, text_query,
    )
    return text_part(vis_query.shape, *held)


def solution(mesh):
    placed = (
        P("group", "seq", None),
        P("group", "seq", None),
        P("group", "seq", None),
        P("group", "seq", None),
        P(),
        P("group"),
        P(),
        P(("group", "seq"), None),
        P(("group", "seq")),
    )
    return jax.shard_map(
        functools.partial(on_device, mesh.shape["seq"]),
        mesh=mesh,
        in_specs=placed,
        out_specs=(P("group", "seq", None), P(("group", "seq"), None)),
        check_vma=False,
    )
```

```python
import functools
import math

import jax
import jax.numpy as jnp
from jax import lax
from jax.experimental import pallas as pl
from jax.experimental.pallas import tpu as pltpu
from jax.sharding import PartitionSpec as P

VHEADS = 16
VHEAD = 80
KVH = 8
HD = 128
QGROUP = 6
TILES = 4
LANES = 128
NEG = -1e30


def vision_attend(query, keys, values, tile_count, nheads):
    images, rows, width = query.shape
    length = keys.shape[1]
    patch = length // TILES
    tile_of = jnp.arange(length, dtype=jnp.int32) // patch
    key_ok = tile_of[None, :] < tile_count[:, None]
    query = query.reshape(images, rows, nheads, VHEAD)
    keys = keys.reshape(images, length, nheads, VHEAD)
    values = values.reshape(images, length, nheads, VHEAD)
    scores = jnp.einsum(
        "bqhd,bkhd->bhqk", query, keys, preferred_element_type=jnp.float32
    ) / math.sqrt(VHEAD)
    scores = jnp.where(key_ok[:, None, None, :], scores, NEG)
    peak = jnp.max(scores, axis=-1, keepdims=True)
    expo = jnp.exp(scores - peak)
    probs = (expo / jnp.sum(expo, axis=-1, keepdims=True)).astype(jnp.bfloat16)
    attn = jnp.einsum("bhqk,bkhd->bqhd", probs, values, preferred_element_type=jnp.float32)
    return attn.reshape(images, rows, width)


def general_form(
    vis_query, vis_key, vis_value, vis_resid, attn_gate, tile_count, w_kv, text_query, text_image
):
    images, rows, width = vis_query.shape
    keys, values = (
        lax.all_gather(vis_key, "seq", axis=1, tiled=True),
        lax.all_gather(vis_value, "seq", axis=1, tiled=True),
    )
    attn = vision_attend(vis_query, keys, values, tile_count, VHEADS)
    vision_out = (vis_resid.astype(jnp.float32) + jnp.tanh(attn_gate[0]) * attn).astype(
        jnp.bfloat16
    )
    local_kv = jnp.dot(
        vision_out.reshape(images * rows, width), w_kv, preferred_element_type=jnp.float32
    )
    local_kv = local_kv.astype(jnp.bfloat16).reshape(images, rows, w_kv.shape[1])
    cross_kv = lax.all_gather(local_kv, "seq", axis=1, tiled=True)
    length = cross_kv.shape[1]
    patch = length // TILES
    tile_of = jnp.arange(length, dtype=jnp.int32) // patch
    key_ok = tile_of[None, :] < tile_count[:, None]
    half = KVH * HD
    flat_kv = cross_kv.reshape(images * length, 2 * half)
    cross_key = flat_kv[:, :half].reshape(images * length, KVH, HD)
    cross_value = flat_kv[:, half:].reshape(images * length, KVH, HD)
    image_of_key = jnp.arange(images * length, dtype=jnp.int32) // length
    flat_ok = key_ok.reshape(images * length)
    tokens = text_query.shape[0]
    qrows = text_query.reshape(tokens, KVH, QGROUP, HD)
    score = jnp.einsum(
        "tgqd,kgd->tgqk", qrows, cross_key, preferred_element_type=jnp.float32
    ) / math.sqrt(HD)
    allowed = (image_of_key[None, :] <= text_image[:, None]) & flat_ok[None, :]
    score = jnp.where(allowed[:, None, None, :], score, NEG)
    top = jnp.max(score, axis=-1, keepdims=True)
    expd = jnp.exp(score - top)
    prob = (expd / jnp.sum(expd, axis=-1, keepdims=True)).astype(jnp.bfloat16)
    out = jnp.einsum("tgqk,kgd->tgqd", prob, cross_value, preferred_element_type=jnp.float32)
    cross_out = out.reshape(tokens, KVH * QGROUP * HD).astype(jnp.bfloat16)
    return (vision_out, cross_out)


GRANT = 16 * 1024 * 1024
MESH = pl.DeviceIdType.MESH
CORES = 2


def gather_kernel(
    n, images, rows, width, tokens,
    gate_in, count_in, seen_in, q_in, k_in, v_in, r_in, w_in, text_in,
    vis_ref, bias_ref, pick_ref, kv_ref, text_ref,
    w_ref, other, slots, seen_ref, gate_ref, count_ref,
    load_sem, small_sem, big_sem, send_sem, recv_sem, swap_sem,
):
    me = lax.axis_index("seq")
    chip, core = me // CORES, me % CORES
    row, col = chip // 2, chip % 2
    partner = chip * CORES + (1 - core)
    across = row * 2 + (1 - col)
    along = (1 - row) * 2 + col
    corner = (1 - row) * 2 + (1 - col)
    length = n * rows
    keys = images * length

    sources = (q_in, k_in, v_in, r_in)
    mine = slots.at[me]
    loads = [
        pltpu.make_async_copy(ref.at[image], into.at[a], load_sem)
        for a, ref in enumerate(sources)
        for image, into in ((core, mine), (1 - core, other))
    ]

    def all_of(ref, sem):
        return pltpu.make_async_copy(ref, ref, sem)

    barrier = pltpu.get_barrier_semaphore()
    chips = (corner, across, along)
    others = [there * CORES + b for there in chips for b in range(CORES)] + [partner]
    for dev in others:
        pl.semaphore_signal(barrier, inc=1, device_id={"seq": dev}, device_id_type=MESH)
    for load in loads:
        load.start()
    small = [
        pltpu.make_async_copy(gate_in, gate_ref, small_sem.at[0]),
        pltpu.make_async_copy(count_in, count_ref, small_sem.at[1]),
        pltpu.make_async_copy(seen_in, seen_ref, small_sem.at[2]),
    ]
    big = [
        pltpu.make_async_copy(w_in, w_ref, big_sem.at[0]),
        pltpu.make_async_copy(text_in, text_ref, big_sem.at[1]),
    ]
    for copy in small:
        copy.start()
    pl.semaphore_wait(barrier, len(others))
    all_of(slots.at[:2], load_sem).wait()

    cuts = (pl.ds(0, 3), pl.ds(3, 1))

    def send(src, part, dev):
        pltpu.make_async_remote_copy(
            src_ref=src.at[cuts[part]],
            dst_ref=slots.at[me, cuts[part]],
            send_sem=send_sem,
            recv_sem=recv_sem.at[part],
            device_id={"seq": dev},
            device_id_type=MESH,
        ).start()

    for part in range(2):
        for there in chips:
            send(mine, part, there * CORES + core)
            send(other, part, there * CORES + 1 - core)
        send(other, part, partner)
    for copy in big:
        copy.start()

    for copy in small:
        copy.wait()
    place = lax.broadcasted_iota(jnp.int32, (length, tokens), 0)
    for b in range(images):
        ok = (place // (length // TILES) < count_ref[b]) & (seen_ref[...] >= b)
        bias = jnp.where(ok, 0.0, NEG)
        for twin in range(2):
            at = twin * keys + b * length
            bias_ref[at : at + length, :] = bias
    line = lax.broadcasted_iota(jnp.int32, pick_ref.shape, 0)
    want = (line // 8) * length + me * rows + line % 8
    key_at = lax.broadcasted_iota(jnp.int32, pick_ref.shape, 1)
    pick_ref[...] = jnp.where(key_at == want, 1.0, 0.0).astype(jnp.bfloat16)
    gate = jnp.tanh(jnp.full((1, LANES), gate_ref[0], jnp.float32))

    def arrived(part):
        all_of(slots.at[: n - 1, cuts[part]], recv_sem.at[part]).wait()

    def whole(a):
        return jnp.concatenate(
            [slots[s, a].astype(jnp.float32) for s in range(n)], axis=0
        )

    arrived(0)
    query, key, value = (whole(a).astype(jnp.bfloat16) for a in range(3))
    heads = width // VHEAD
    side = LANES // length
    groups = range(0, heads, side)
    key_row = lax.broadcasted_iota(jnp.int32, (length, LANES), 0)
    scale = math.log2(math.e) / math.sqrt(VHEAD)
    count = jnp.where(core == 0, count_ref[0], count_ref[1])
    bias = jnp.where(key_row // (length // TILES) < count, 0.0, NEG)
    windows, owners, scores = [], [], []
    for h in groups:
        lo, hi = h * VHEAD // LANES * LANES, -(-(h + side) * VHEAD // LANES) * LANES
        lane = lax.broadcasted_iota(jnp.int32, (length, hi - lo), 1) + lo
        masks = [(lane >= i * VHEAD) & (lane < (i + 1) * VHEAD) for i in range(h, h + side)]
        window = query[:, lo:hi]
        spread = jnp.concatenate(
            [jnp.where(mask, window, jnp.zeros_like(window)) for mask in masks], axis=0
        )
        score = lax.dot_general(
            key[:, lo:hi], spread, (((1,), (1,)), ((), ())),
            preferred_element_type=jnp.float32,
        )
        windows.append((lo, hi))
        owners.append(masks)
        scores.append(score + bias)
    probs = []
    for score in scores:
        expo = jnp.exp2((score - jnp.max(score, axis=0, keepdims=True)) * scale)
        prob = expo * (1.0 / jnp.sum(expo, axis=0, keepdims=True))
        probs.append(prob.astype(jnp.bfloat16))
    parts = [None] * (width // LANES)
    for (lo, hi), masks, prob in zip(windows, owners, probs):
        attn = lax.dot_general(
            prob, value[:, lo:hi], (((0,), (0,)), ((), ())),
            preferred_element_type=jnp.float32,
        )
        total = jnp.zeros((length, hi - lo), jnp.float32)
        for i, mask in enumerate(masks):
            total = jnp.where(mask, attn[i * length : (i + 1) * length], total)
        for t in range(lo // LANES, hi // LANES):
            piece = total[:, t * LANES - lo : (t + 1) * LANES - lo]
            parts[t] = piece if parts[t] is None else parts[t] + piece
    branch = jnp.concatenate(parts, axis=1) * jnp.tile(gate, (1, len(parts)))
    arrived(1)
    here = pl.ds(pl.multiple_of(core * length, length), length)
    vis_ref[here, :] = (whole(3) + branch).astype(jnp.bfloat16)

    there = pl.ds(pl.multiple_of((1 - core) * length, length), length)
    half = KVH * HD

    def swap(ref, at, number):
        return pltpu.make_async_remote_copy(
            src_ref=ref.at[at],
            dst_ref=ref.at[at],
            send_sem=swap_sem.at[number],
            recv_sem=swap_sem.at[number + 1],
            device_id={"seq": partner},
            device_id_type=MESH,
        )

    def project(at, first, last):
        vis = vis_ref[at, :]
        for start in range(first, last, 2 * HD):
            cols = slice(start, start + 2 * HD)
            kv_ref[at, cols] = jnp.dot(
                vis, w_ref[:, cols], preferred_element_type=jnp.float32
            ).astype(jnp.bfloat16)

    vis_swap = swap(vis_ref, here, 0)
    key_swap = swap(kv_ref, (here, pl.ds(0, half)), 2)
    vis_swap.start()
    for copy in big:
        copy.wait()
    project(here, 0, half)
    key_swap.start()
    project(here, half, 2 * half)
    swap(vis_ref, there, 0).wait_recv()
    project(there, half, 2 * half)
    all_of(slots.at[: n - 1], send_sem).wait()
    vis_swap.wait_send()
    key_swap.wait_send()
    swap(kv_ref, (there, pl.ds(0, half)), 2).wait_recv()


def gather_part(n, q, k, v, r, gate, count, seen, w_kv, text):
    images, rows, width = q.shape
    length = n * rows
    keys = images * length
    tokens = seen.shape[0]
    hbm = pl.BlockSpec(memory_space=pltpu.HBM)
    vmem = pl.BlockSpec(memory_space=pltpu.VMEM)
    held = [
        pltpu.with_memory_space_constraint(x, pltpu.HBM)
        for x in (count, seen.reshape(1, tokens), q, k, v, r, w_kv, text)
    ]
    return pl.pallas_call(
        functools.partial(gather_kernel, n, images, rows, width, tokens),
        out_shape=(
            jax.ShapeDtypeStruct((keys, width), jnp.bfloat16),
            jax.ShapeDtypeStruct((2 * keys, tokens), jnp.float32),
            jax.ShapeDtypeStruct((8 * images, keys), jnp.bfloat16),
            jax.ShapeDtypeStruct((keys, w_kv.shape[1]), jnp.bfloat16),
            jax.ShapeDtypeStruct(text.shape, jnp.bfloat16),
        ),
        in_specs=[hbm] * 9,
        out_specs=(vmem,) * 5,
        scratch_shapes=[
            pltpu.VMEM(w_kv.shape, jnp.bfloat16),
            pltpu.VMEM((4, rows, width), jnp.bfloat16),
            pltpu.VMEM((n, 4, rows, width), jnp.bfloat16),
            pltpu.VMEM((1, tokens), jnp.int32),
            pltpu.SMEM((1,), jnp.float32),
            pltpu.SMEM((images,), jnp.int32),
            pltpu.SemaphoreType.DMA,
            pltpu.SemaphoreType.DMA((3,)),
            pltpu.SemaphoreType.DMA((2,)),
            pltpu.SemaphoreType.DMA,
            pltpu.SemaphoreType.DMA((2,)),
            pltpu.SemaphoreType.DMA((4,)),
        ],
        compiler_params=pltpu.CompilerParams(
            collective_id=0, has_side_effects=True, vmem_limit_bytes=GRANT
        ),
        name="vision",
    )(gate, *held)


def text_kernel(
    vis_ref, bias_ref, pick_ref, kv_ref, q_ref,
    vis_out, out_hbm,
    local_ref, o_ref, local_sem, out_sem,
):
    images, rows, width = local_ref.shape
    keys = vis_ref.shape[0]
    half = KVH * HD
    scale = math.log2(math.e) / math.sqrt(HD)
    span = QGROUP * HD

    def double(x):
        zero = jnp.zeros_like(x)
        return jnp.concatenate(
            [jnp.concatenate([x, zero], axis=1), jnp.concatenate([zero, x], axis=1)], axis=0
        )

    def attend(g, k_two, v_two):
        pairs = QGROUP // 2
        wide = 2 * HD
        scores = [
            lax.dot_general(
                k_two, q_ref[:, g * span + j * wide : g * span + (j + 1) * wide],
                (((1,), (1,)), ((), ())), preferred_element_type=jnp.float32,
            )
            for j in range(pairs)
        ]
        bias = bias_ref[:keys, :]
        probs = []
        for score in scores:
            halves = []
            for part in (score[:keys], score[keys:]):
                part = part + bias
                expd = jnp.exp2((part - jnp.max(part, axis=0, keepdims=True)) * scale)
                halves.append(expd * (1.0 / jnp.sum(expd, axis=0, keepdims=True)))
            probs.append(jnp.concatenate(halves, axis=0).astype(jnp.bfloat16))
        out = lax.dot_general(
            jnp.concatenate(probs, axis=1), v_two, (((0,), (0,)), ((), ())),
            preferred_element_type=jnp.float32,
        ).astype(jnp.bfloat16)
        tokens = out.shape[0] // pairs
        for j in range(pairs):
            o_ref[:, g * span + j * wide : g * span + (j + 1) * wide] = out[
                j * tokens : (j + 1) * tokens
            ]
        cols = pl.ds(g * span, span)
        pltpu.make_async_copy(o_ref.at[:, cols], out_hbm.at[:, cols], out_sem).start()

    local = jnp.dot(pick_ref[...], vis_ref[...], preferred_element_type=jnp.float32)
    for b in range(images):
        local_ref[b] = local[8 * b : 8 * b + rows].astype(jnp.bfloat16)
    local_copy = pltpu.make_async_copy(local_ref, vis_out, local_sem)
    local_copy.start()
    for g in range(KVH):
        attend(
            g,
            double(kv_ref[:, g * HD : (g + 1) * HD]),
            double(kv_ref[:, half + g * HD : half + (g + 1) * HD]),
        )
    local_copy.wait()
    pltpu.make_async_copy(o_ref, out_hbm, out_sem).wait()


def text_part(shape, vis, bias, pick, kv, query):
    vmem = pl.BlockSpec(memory_space=pltpu.VMEM)
    anyspace = pl.BlockSpec(memory_space=pl.ANY)
    return pl.pallas_call(
        text_kernel,
        out_shape=(
            jax.ShapeDtypeStruct(shape, jnp.bfloat16),
            jax.ShapeDtypeStruct(query.shape, jnp.bfloat16),
        ),
        in_specs=[vmem] * 5,
        out_specs=(anyspace, anyspace),
        scratch_shapes=[
            pltpu.VMEM(shape, jnp.bfloat16),
            pltpu.VMEM(query.shape, jnp.bfloat16),
            pltpu.SemaphoreType.DMA,
            pltpu.SemaphoreType.DMA,
        ],
        compiler_params=pltpu.CompilerParams(vmem_limit_bytes=GRANT),
        name="text",
    )(vis, bias, pick, kv, query)


def fits(n, images, rows, width):
    length = n * rows
    return (
        n == 4 * CORES
        and images == CORES
        and 2 * images * length == LANES
        and LANES % length == 0
        and (width // VHEAD) % (LANES // length) == 0
        and rows <= 8
        and length % 16 == 0
    )


def on_device(n, *args):
    vis_query, vis_key, vis_value, vis_resid, attn_gate, tile_count, w_kv, text_query, text_image = args
    images, rows, width = vis_query.shape
    if not fits(n, images, rows, width):
        return general_form(*args)
    held = gather_part(
        n, vis_query, vis_key, vis_value, vis_resid, attn_gate, tile_count, text_image,
        w_kv, text_query,
    )
    return text_part(vis_query.shape, *held)


def solution(mesh):
    placed = (
        P("group", "seq", None),
        P("group", "seq", None),
        P("group", "seq", None),
        P("group", "seq", None),
        P(),
        P("group"),
        P(),
        P(("group", "seq"), None),
        P(("group", "seq")),
    )
    return jax.shard_map(
        functools.partial(on_device, mesh.shape["seq"]),
        mesh=mesh,
        in_specs=placed,
        out_specs=(P("group", "seq", None), P(("group", "seq"), None)),
        check_vma=False,
    )
```

```python
import functools
import math

import jax
import jax.numpy as jnp
from jax import lax
from jax.experimental import pallas as pl
from jax.experimental.pallas import tpu as pltpu
from jax.sharding import PartitionSpec as P

VHEADS = 16
VHEAD = 80
KVH = 8
HD = 128
QGROUP = 6
TILES = 4
LANES = 128
NEG = -1e30


def vision_attend(query, keys, values, tile_count, nheads):
    images, rows, width = query.shape
    length = keys.shape[1]
    patch = length // TILES
    tile_of = jnp.arange(length, dtype=jnp.int32) // patch
    key_ok = tile_of[None, :] < tile_count[:, None]
    query = query.reshape(images, rows, nheads, VHEAD)
    keys = keys.reshape(images, length, nheads, VHEAD)
    values = values.reshape(images, length, nheads, VHEAD)
    scores = jnp.einsum(
        "bqhd,bkhd->bhqk", query, keys, preferred_element_type=jnp.float32
    ) / math.sqrt(VHEAD)
    scores = jnp.where(key_ok[:, None, None, :], scores, NEG)
    peak = jnp.max(scores, axis=-1, keepdims=True)
    expo = jnp.exp(scores - peak)
    probs = (expo / jnp.sum(expo, axis=-1, keepdims=True)).astype(jnp.bfloat16)
    attn = jnp.einsum("bhqk,bkhd->bqhd", probs, values, preferred_element_type=jnp.float32)
    return attn.reshape(images, rows, width)


def general_form(
    vis_query, vis_key, vis_value, vis_resid, attn_gate, tile_count, w_kv, text_query, text_image
):
    images, rows, width = vis_query.shape
    keys, values = (
        lax.all_gather(vis_key, "seq", axis=1, tiled=True),
        lax.all_gather(vis_value, "seq", axis=1, tiled=True),
    )
    attn = vision_attend(vis_query, keys, values, tile_count, VHEADS)
    vision_out = (vis_resid.astype(jnp.float32) + jnp.tanh(attn_gate[0]) * attn).astype(
        jnp.bfloat16
    )
    local_kv = jnp.dot(
        vision_out.reshape(images * rows, width), w_kv, preferred_element_type=jnp.float32
    )
    local_kv = local_kv.astype(jnp.bfloat16).reshape(images, rows, w_kv.shape[1])
    cross_kv = lax.all_gather(local_kv, "seq", axis=1, tiled=True)
    length = cross_kv.shape[1]
    patch = length // TILES
    tile_of = jnp.arange(length, dtype=jnp.int32) // patch
    key_ok = tile_of[None, :] < tile_count[:, None]
    half = KVH * HD
    flat_kv = cross_kv.reshape(images * length, 2 * half)
    cross_key = flat_kv[:, :half].reshape(images * length, KVH, HD)
    cross_value = flat_kv[:, half:].reshape(images * length, KVH, HD)
    image_of_key = jnp.arange(images * length, dtype=jnp.int32) // length
    flat_ok = key_ok.reshape(images * length)
    tokens = text_query.shape[0]
    qrows = text_query.reshape(tokens, KVH, QGROUP, HD)
    score = jnp.einsum(
        "tgqd,kgd->tgqk", qrows, cross_key, preferred_element_type=jnp.float32
    ) / math.sqrt(HD)
    allowed = (image_of_key[None, :] <= text_image[:, None]) & flat_ok[None, :]
    score = jnp.where(allowed[:, None, None, :], score, NEG)
    top = jnp.max(score, axis=-1, keepdims=True)
    expd = jnp.exp(score - top)
    prob = (expd / jnp.sum(expd, axis=-1, keepdims=True)).astype(jnp.bfloat16)
    out = jnp.einsum("tgqk,kgd->tgqd", prob, cross_value, preferred_element_type=jnp.float32)
    cross_out = out.reshape(tokens, KVH * QGROUP * HD).astype(jnp.bfloat16)
    return (vision_out, cross_out)


GRANT = 16 * 1024 * 1024
MESH = pl.DeviceIdType.MESH
CORES = 2


def gather_kernel(
    n, images, rows, width, tokens,
    gate_in, count_in, seen_in, q_in, k_in, v_in, r_in, w_in, text_in,
    vis_ref, bias_ref, pick_ref, kv_ref, text_ref,
    w_ref, other, slots, seen_ref, gate_ref, count_ref,
    load_sem, small_sem, big_sem, send_sem, recv_sem, swap_sem,
):
    me = lax.axis_index("seq")
    chip, core = me // CORES, me % CORES
    row, col = chip // 2, chip % 2
    partner = chip * CORES + (1 - core)
    across = row * 2 + (1 - col)
    along = (1 - row) * 2 + col
    corner = (1 - row) * 2 + (1 - col)
    length = n * rows
    keys = images * length

    sources = (q_in, k_in, v_in, r_in)
    mine = slots.at[me]
    loads = [
        pltpu.make_async_copy(ref.at[image], into.at[a], load_sem)
        for a, ref in enumerate(sources)
        for image, into in ((core, mine), (1 - core, other))
    ]

    def all_of(ref, sem):
        return pltpu.make_async_copy(ref, ref, sem)

    barrier = pltpu.get_barrier_semaphore()
    chips = (corner, across, along)
    others = [there * CORES + b for there in chips for b in range(CORES)] + [partner]
    for dev in others:
        pl.semaphore_signal(barrier, inc=1, device_id={"seq": dev}, device_id_type=MESH)
    for load in loads:
        load.start()
    small = [
        pltpu.make_async_copy(gate_in, gate_ref, small_sem.at[0]),
        pltpu.make_async_copy(count_in, count_ref, small_sem.at[1]),
        pltpu.make_async_copy(seen_in, seen_ref, small_sem.at[2]),
    ]
    big = [
        pltpu.make_async_copy(w_in, w_ref, big_sem.at[0]),
        pltpu.make_async_copy(text_in, text_ref, big_sem.at[1]),
    ]
    for copy in small:
        copy.start()
    pl.semaphore_wait(barrier, len(others))
    all_of(slots.at[:2], load_sem).wait()

    cuts = (pl.ds(0, 3), pl.ds(3, 1))

    def send(src, part, dev):
        pltpu.make_async_remote_copy(
            src_ref=src.at[cuts[part]],
            dst_ref=slots.at[me, cuts[part]],
            send_sem=send_sem,
            recv_sem=recv_sem.at[part],
            device_id={"seq": dev},
            device_id_type=MESH,
        ).start()

    for part in range(2):
        for there in chips:
            send(mine, part, there * CORES + core)
            send(other, part, there * CORES + 1 - core)
        send(other, part, partner)
    for copy in big:
        copy.start()

    for copy in small:
        copy.wait()
    place = lax.broadcasted_iota(jnp.int32, (length, tokens), 0)
    for b in range(images):
        ok = (place // (length // TILES) < count_ref[b]) & (seen_ref[...] >= b)
        bias = jnp.where(ok, 0.0, NEG)
        for twin in range(2):
            at = twin * keys + b * length
            bias_ref[at : at + length, :] = bias
    line = lax.broadcasted_iota(jnp.int32, pick_ref.shape, 0)
    want = (line // 8) * length + me * rows + line % 8
    key_at = lax.broadcasted_iota(jnp.int32, pick_ref.shape, 1)
    pick_ref[...] = jnp.where(key_at == want, 1.0, 0.0).astype(jnp.bfloat16)
    gate = jnp.tanh(jnp.full((1, LANES), gate_ref[0], jnp.float32))

    def arrived(part):
        all_of(slots.at[: n - 1, cuts[part]], recv_sem.at[part]).wait()

    def whole(a):
        return jnp.concatenate(
            [slots[s, a].astype(jnp.float32) for s in range(n)], axis=0
        )

    arrived(0)
    query, key, value = (whole(a).astype(jnp.bfloat16) for a in range(3))
    heads = width // VHEAD
    side = LANES // length
    groups = range(0, heads, side)
    key_row = lax.broadcasted_iota(jnp.int32, (length, LANES), 0)
    scale = math.log2(math.e) / math.sqrt(VHEAD)
    count = jnp.where(core == 0, count_ref[0], count_ref[1])
    bias = jnp.where(key_row // (length // TILES) < count, 0.0, NEG)
    windows, owners, scores = [], [], []
    for h in groups:
        lo, hi = h * VHEAD // LANES * LANES, -(-(h + side) * VHEAD // LANES) * LANES
        lane = lax.broadcasted_iota(jnp.int32, (length, hi - lo), 1) + lo
        masks = [(lane >= i * VHEAD) & (lane < (i + 1) * VHEAD) for i in range(h, h + side)]
        window = query[:, lo:hi]
        spread = jnp.concatenate(
            [jnp.where(mask, window, jnp.zeros_like(window)) for mask in masks], axis=0
        )
        score = lax.dot_general(
            key[:, lo:hi], spread, (((1,), (1,)), ((), ())),
            preferred_element_type=jnp.float32,
        )
        windows.append((lo, hi))
        owners.append(masks)
        scores.append(score + bias)
    probs = []
    for score in scores:
        expo = jnp.exp2((score - jnp.max(score, axis=0, keepdims=True)) * scale)
        prob = expo * (1.0 / jnp.sum(expo, axis=0, keepdims=True))
        probs.append(prob.astype(jnp.bfloat16))
    parts = [None] * (width // LANES)
    for (lo, hi), masks, prob in zip(windows, owners, probs):
        attn = lax.dot_general(
            prob, value[:, lo:hi], (((0,), (0,)), ((), ())),
            preferred_element_type=jnp.float32,
        )
        total = jnp.zeros((length, hi - lo), jnp.float32)
        for i, mask in enumerate(masks):
            total = jnp.where(mask, attn[i * length : (i + 1) * length], total)
        for t in range(lo // LANES, hi // LANES):
            piece = total[:, t * LANES - lo : (t + 1) * LANES - lo]
            parts[t] = piece if parts[t] is None else parts[t] + piece
    branch = jnp.concatenate(parts, axis=1) * jnp.tile(gate, (1, len(parts)))
    arrived(1)
    here = pl.ds(pl.multiple_of(core * length, length), length)
    vis_ref[here, :] = (whole(3) + branch).astype(jnp.bfloat16)

    there = pl.ds(pl.multiple_of((1 - core) * length, length), length)
    half = KVH * HD

    def swap(ref, at, number):
        return pltpu.make_async_remote_copy(
            src_ref=ref.at[at],
            dst_ref=ref.at[at],
            send_sem=swap_sem.at[number],
            recv_sem=swap_sem.at[number + 1],
            device_id={"seq": partner},
            device_id_type=MESH,
        )

    def project(at, first, last):
        vis = vis_ref[at, :]
        for start in range(first, last, 2 * HD):
            cols = slice(start, start + 2 * HD)
            kv_ref[at, cols] = jnp.dot(
                vis, w_ref[:, cols], preferred_element_type=jnp.float32
            ).astype(jnp.bfloat16)

    vis_swap = swap(vis_ref, here, 0)
    key_swap = swap(kv_ref, (here, pl.ds(0, half)), 2)
    vis_swap.start()
    for copy in big:
        copy.wait()
    project(here, 0, half)
    key_swap.start()
    swap(vis_ref, there, 0).wait_recv()
    project(pl.ds(0, keys), half, 2 * half)
    all_of(slots.at[: n - 1], send_sem).wait()
    vis_swap.wait_send()
    key_swap.wait_send()
    swap(kv_ref, (there, pl.ds(0, half)), 2).wait_recv()


def gather_part(n, q, k, v, r, gate, count, seen, w_kv, text):
    images, rows, width = q.shape
    length = n * rows
    keys = images * length
    tokens = seen.shape[0]
    hbm = pl.BlockSpec(memory_space=pltpu.HBM)
    vmem = pl.BlockSpec(memory_space=pltpu.VMEM)
    held = [
        pltpu.with_memory_space_constraint(x, pltpu.HBM)
        for x in (count, seen.reshape(1, tokens), q, k, v, r, w_kv, text)
    ]
    return pl.pallas_call(
        functools.partial(gather_kernel, n, images, rows, width, tokens),
        out_shape=(
            jax.ShapeDtypeStruct((keys, width), jnp.bfloat16),
            jax.ShapeDtypeStruct((2 * keys, tokens), jnp.float32),
            jax.ShapeDtypeStruct((8 * images, keys), jnp.bfloat16),
            jax.ShapeDtypeStruct((keys, w_kv.shape[1]), jnp.bfloat16),
            jax.ShapeDtypeStruct(text.shape, jnp.bfloat16),
        ),
        in_specs=[hbm] * 9,
        out_specs=(vmem,) * 5,
        scratch_shapes=[
            pltpu.VMEM(w_kv.shape, jnp.bfloat16),
            pltpu.VMEM((4, rows, width), jnp.bfloat16),
            pltpu.VMEM((n, 4, rows, width), jnp.bfloat16),
            pltpu.VMEM((1, tokens), jnp.int32),
            pltpu.SMEM((1,), jnp.float32),
            pltpu.SMEM((images,), jnp.int32),
            pltpu.SemaphoreType.DMA,
            pltpu.SemaphoreType.DMA((3,)),
            pltpu.SemaphoreType.DMA((2,)),
            pltpu.SemaphoreType.DMA,
            pltpu.SemaphoreType.DMA((2,)),
            pltpu.SemaphoreType.DMA((4,)),
        ],
        compiler_params=pltpu.CompilerParams(
            collective_id=0, has_side_effects=True, vmem_limit_bytes=GRANT
        ),
        name="vision",
    )(gate, *held)


def text_kernel(
    vis_ref, bias_ref, pick_ref, kv_ref, q_ref,
    vis_out, out_hbm,
    local_ref, o_ref, local_sem, out_sem,
):
    images, rows, width = local_ref.shape
    keys = vis_ref.shape[0]
    half = KVH * HD
    scale = math.log2(math.e) / math.sqrt(HD)
    span = QGROUP * HD

    def double(x):
        zero = jnp.zeros_like(x)
        return jnp.concatenate(
            [jnp.concatenate([x, zero], axis=1), jnp.concatenate([zero, x], axis=1)], axis=0
        )

    def attend(g, k_two, v_two):
        pairs = QGROUP // 2
        wide = 2 * HD
        scores = [
            lax.dot_general(
                k_two, q_ref[:, g * span + j * wide : g * span + (j + 1) * wide],
                (((1,), (1,)), ((), ())), preferred_element_type=jnp.float32,
            )
            for j in range(pairs)
        ]
        bias = bias_ref[:keys, :]
        probs = []
        for score in scores:
            halves = []
            for part in (score[:keys], score[keys:]):
                part = part + bias
                expd = jnp.exp2((part - jnp.max(part, axis=0, keepdims=True)) * scale)
                halves.append(expd * (1.0 / jnp.sum(expd, axis=0, keepdims=True)))
            probs.append(jnp.concatenate(halves, axis=0).astype(jnp.bfloat16))
        parts = [probs] if g < KVH - 1 else [[prob] for prob in probs]
        j = 0
        for part in parts:
            out = lax.dot_general(
                jnp.concatenate(part, axis=1), v_two, (((0,), (0,)), ((), ())),
                preferred_element_type=jnp.float32,
            ).astype(jnp.bfloat16)
            tokens = out.shape[0] // len(part)
            for i in range(len(part)):
                at = g * span + j * wide
                o_ref[:, at : at + wide] = out[i * tokens : (i + 1) * tokens]
                j += 1
        cols = pl.ds(g * span, span)
        pltpu.make_async_copy(o_ref.at[:, cols], out_hbm.at[:, cols], out_sem).start()

    local = jnp.dot(pick_ref[...], vis_ref[...], preferred_element_type=jnp.float32)
    for b in range(images):
        local_ref[b] = local[8 * b : 8 * b + rows].astype(jnp.bfloat16)
    local_copy = pltpu.make_async_copy(local_ref, vis_out, local_sem)
    local_copy.start()
    for g in range(KVH):
        attend(
            g,
            double(kv_ref[:, g * HD : (g + 1) * HD]),
            double(kv_ref[:, half + g * HD : half + (g + 1) * HD]),
        )
    local_copy.wait()
    pltpu.make_async_copy(o_ref, out_hbm, out_sem).wait()


def text_part(shape, vis, bias, pick, kv, query):
    vmem = pl.BlockSpec(memory_space=pltpu.VMEM)
    anyspace = pl.BlockSpec(memory_space=pl.ANY)
    return pl.pallas_call(
        text_kernel,
        out_shape=(
            jax.ShapeDtypeStruct(shape, jnp.bfloat16),
            jax.ShapeDtypeStruct(query.shape, jnp.bfloat16),
        ),
        in_specs=[vmem] * 5,
        out_specs=(anyspace, anyspace),
        scratch_shapes=[
            pltpu.VMEM(shape, jnp.bfloat16),
            pltpu.VMEM(query.shape, jnp.bfloat16),
            pltpu.SemaphoreType.DMA,
            pltpu.SemaphoreType.DMA,
        ],
        compiler_params=pltpu.CompilerParams(vmem_limit_bytes=GRANT),
        name="text",
    )(vis, bias, pick, kv, query)


def fits(n, images, rows, width):
    length = n * rows
    return (
        n == 4 * CORES
        and images == CORES
        and 2 * images * length == LANES
        and LANES % length == 0
        and (width // VHEAD) % (LANES // length) == 0
        and rows <= 8
        and length % 16 == 0
    )


def on_device(n, *args):
    vis_query, vis_key, vis_value, vis_resid, attn_gate, tile_count, w_kv, text_query, text_image = args
    images, rows, width = vis_query.shape
    if not fits(n, images, rows, width):
        return general_form(*args)
    held = gather_part(
        n, vis_query, vis_key, vis_value, vis_resid, attn_gate, tile_count, text_image,
        w_kv, text_query,
    )
    return text_part(vis_query.shape, *held)


def solution(mesh):
    placed = (
        P("group", "seq", None),
        P("group", "seq", None),
        P("group", "seq", None),
        P("group", "seq", None),
        P(),
        P("group"),
        P(),
        P(("group", "seq"), None),
        P(("group", "seq")),
    )
    return jax.shard_map(
        functools.partial(on_device, mesh.shape["seq"]),
        mesh=mesh,
        in_specs=placed,
        out_specs=(P("group", "seq", None), P(("group", "seq"), None)),
        check_vma=False,
    )
```

```python
import functools
import math

import jax
import jax.numpy as jnp
from jax import lax
from jax.experimental import pallas as pl
from jax.experimental.pallas import tpu as pltpu
from jax.sharding import PartitionSpec as P

VHEADS = 16
VHEAD = 80
KVH = 8
HD = 128
QGROUP = 6
TILES = 4
LANES = 128
NEG = -1e30


def vision_attend(query, keys, values, tile_count, nheads):
    images, rows, width = query.shape
    length = keys.shape[1]
    patch = length // TILES
    tile_of = jnp.arange(length, dtype=jnp.int32) // patch
    key_ok = tile_of[None, :] < tile_count[:, None]
    query = query.reshape(images, rows, nheads, VHEAD)
    keys = keys.reshape(images, length, nheads, VHEAD)
    values = values.reshape(images, length, nheads, VHEAD)
    scores = jnp.einsum(
        "bqhd,bkhd->bhqk", query, keys, preferred_element_type=jnp.float32
    ) / math.sqrt(VHEAD)
    scores = jnp.where(key_ok[:, None, None, :], scores, NEG)
    peak = jnp.max(scores, axis=-1, keepdims=True)
    expo = jnp.exp(scores - peak)
    probs = (expo / jnp.sum(expo, axis=-1, keepdims=True)).astype(jnp.bfloat16)
    attn = jnp.einsum("bhqk,bkhd->bqhd", probs, values, preferred_element_type=jnp.float32)
    return attn.reshape(images, rows, width)


def general_form(
    vis_query, vis_key, vis_value, vis_resid, attn_gate, tile_count, w_kv, text_query, text_image
):
    images, rows, width = vis_query.shape
    keys, values = (
        lax.all_gather(vis_key, "seq", axis=1, tiled=True),
        lax.all_gather(vis_value, "seq", axis=1, tiled=True),
    )
    attn = vision_attend(vis_query, keys, values, tile_count, VHEADS)
    vision_out = (vis_resid.astype(jnp.float32) + jnp.tanh(attn_gate[0]) * attn).astype(
        jnp.bfloat16
    )
    local_kv = jnp.dot(
        vision_out.reshape(images * rows, width), w_kv, preferred_element_type=jnp.float32
    )
    local_kv = local_kv.astype(jnp.bfloat16).reshape(images, rows, w_kv.shape[1])
    cross_kv = lax.all_gather(local_kv, "seq", axis=1, tiled=True)
    length = cross_kv.shape[1]
    patch = length // TILES
    tile_of = jnp.arange(length, dtype=jnp.int32) // patch
    key_ok = tile_of[None, :] < tile_count[:, None]
    half = KVH * HD
    flat_kv = cross_kv.reshape(images * length, 2 * half)
    cross_key = flat_kv[:, :half].reshape(images * length, KVH, HD)
    cross_value = flat_kv[:, half:].reshape(images * length, KVH, HD)
    image_of_key = jnp.arange(images * length, dtype=jnp.int32) // length
    flat_ok = key_ok.reshape(images * length)
    tokens = text_query.shape[0]
    qrows = text_query.reshape(tokens, KVH, QGROUP, HD)
    score = jnp.einsum(
        "tgqd,kgd->tgqk", qrows, cross_key, preferred_element_type=jnp.float32
    ) / math.sqrt(HD)
    allowed = (image_of_key[None, :] <= text_image[:, None]) & flat_ok[None, :]
    score = jnp.where(allowed[:, None, None, :], score, NEG)
    top = jnp.max(score, axis=-1, keepdims=True)
    expd = jnp.exp(score - top)
    prob = (expd / jnp.sum(expd, axis=-1, keepdims=True)).astype(jnp.bfloat16)
    out = jnp.einsum("tgqk,kgd->tgqd", prob, cross_value, preferred_element_type=jnp.float32)
    cross_out = out.reshape(tokens, KVH * QGROUP * HD).astype(jnp.bfloat16)
    return (vision_out, cross_out)


GRANT = 16 * 1024 * 1024
MESH = pl.DeviceIdType.MESH
CORES = 2


def gather_kernel(
    n, images, rows, width, tokens,
    gate_in, count_in, seen_in, q_in, k_in, v_in, r_in, w_in, text_in,
    vis_ref, bias_ref, pick_ref, kv_ref, text_ref,
    w_ref, other, slots, seen_ref, gate_ref, count_ref,
    load_sem, small_sem, big_sem, send_sem, recv_sem, swap_sem,
):
    me = lax.axis_index("seq")
    chip, core = me // CORES, me % CORES
    row, col = chip // 2, chip % 2
    partner = chip * CORES + (1 - core)
    across = row * 2 + (1 - col)
    along = (1 - row) * 2 + col
    corner = (1 - row) * 2 + (1 - col)
    length = n * rows
    keys = images * length

    sources = (q_in, k_in, v_in, r_in)
    mine = slots.at[me]
    loads = [
        pltpu.make_async_copy(ref.at[image], into.at[a], load_sem)
        for a, ref in enumerate(sources)
        for image, into in ((core, mine), (1 - core, other))
    ]

    def all_of(ref, sem):
        return pltpu.make_async_copy(ref, ref, sem)

    barrier = pltpu.get_barrier_semaphore()
    chips = (corner, across, along)
    others = [there * CORES + b for there in chips for b in range(CORES)] + [partner]
    for dev in others:
        pl.semaphore_signal(barrier, inc=1, device_id={"seq": dev}, device_id_type=MESH)
    for load in loads:
        load.start()
    small = [
        pltpu.make_async_copy(gate_in, gate_ref, small_sem.at[0]),
        pltpu.make_async_copy(count_in, count_ref, small_sem.at[1]),
        pltpu.make_async_copy(seen_in, seen_ref, small_sem.at[2]),
    ]
    big = [
        pltpu.make_async_copy(w_in, w_ref, big_sem.at[0]),
        pltpu.make_async_copy(text_in, text_ref, big_sem.at[1]),
    ]
    for copy in small:
        copy.start()
    pl.semaphore_wait(barrier, len(others))
    all_of(slots.at[:2], load_sem).wait()

    cuts = (pl.ds(0, 3), pl.ds(3, 1))

    def send(src, part, dev):
        pltpu.make_async_remote_copy(
            src_ref=src.at[cuts[part]],
            dst_ref=slots.at[me, cuts[part]],
            send_sem=send_sem,
            recv_sem=recv_sem.at[part],
            device_id={"seq": dev},
            device_id_type=MESH,
        ).start()

    for part in range(2):
        for there in chips:
            send(mine, part, there * CORES + core)
            send(other, part, there * CORES + 1 - core)
        send(other, part, partner)
    for copy in big:
        copy.start()

    for copy in small:
        copy.wait()
    place = lax.broadcasted_iota(jnp.int32, (length, tokens), 0)
    for b in range(images):
        ok = (place // (length // TILES) < count_ref[b]) & (seen_ref[...] >= b)
        bias = jnp.where(ok, 0.0, NEG)
        for twin in range(2):
            at = twin * keys + b * length
            bias_ref[at : at + length, :] = bias
    line = lax.broadcasted_iota(jnp.int32, pick_ref.shape, 0)
    want = (line // 8) * length + me * rows + line % 8
    key_at = lax.broadcasted_iota(jnp.int32, pick_ref.shape, 1)
    pick_ref[...] = jnp.where(key_at == want, 1.0, 0.0).astype(jnp.bfloat16)
    gate = jnp.tanh(jnp.full((1, LANES), gate_ref[0], jnp.float32))

    def arrived(part):
        all_of(slots.at[: n - 1, cuts[part]], recv_sem.at[part]).wait()

    def whole(a):
        return jnp.concatenate(
            [slots[s, a].astype(jnp.float32) for s in range(n)], axis=0
        )

    arrived(0)
    query, key, value = (whole(a).astype(jnp.bfloat16) for a in range(3))
    heads = width // VHEAD
    side = LANES // length
    groups = range(0, heads, side)
    key_row = lax.broadcasted_iota(jnp.int32, (length, LANES), 0)
    scale = math.log2(math.e) / math.sqrt(VHEAD)
    count = jnp.where(core == 0, count_ref[0], count_ref[1])
    bias = jnp.where(key_row // (length // TILES) < count, 0.0, NEG)
    windows, owners, scores = [], [], []
    for h in groups:
        lo, hi = h * VHEAD // LANES * LANES, -(-(h + side) * VHEAD // LANES) * LANES
        lane = lax.broadcasted_iota(jnp.int32, (length, hi - lo), 1) + lo
        masks = [(lane >= i * VHEAD) & (lane < (i + 1) * VHEAD) for i in range(h, h + side)]
        window = query[:, lo:hi]
        spread = jnp.concatenate(
            [jnp.where(mask, window, jnp.zeros_like(window)) for mask in masks], axis=0
        )
        score = lax.dot_general(
            key[:, lo:hi], spread, (((1,), (1,)), ((), ())),
            preferred_element_type=jnp.float32,
        )
        windows.append((lo, hi))
        owners.append(masks)
        scores.append(score + bias)
    probs = []
    for score in scores:
        expo = jnp.exp2((score - jnp.max(score, axis=0, keepdims=True)) * scale)
        prob = expo * (1.0 / jnp.sum(expo, axis=0, keepdims=True))
        probs.append(prob.astype(jnp.bfloat16))
    parts = [None] * (width // LANES)
    for (lo, hi), masks, prob in zip(windows, owners, probs):
        attn = lax.dot_general(
            prob, value[:, lo:hi], (((0,), (0,)), ((), ())),
            preferred_element_type=jnp.float32,
        )
        total = jnp.zeros((length, hi - lo), jnp.float32)
        for i, mask in enumerate(masks):
            total = jnp.where(mask, attn[i * length : (i + 1) * length], total)
        for t in range(lo // LANES, hi // LANES):
            piece = total[:, t * LANES - lo : (t + 1) * LANES - lo]
            parts[t] = piece if parts[t] is None else parts[t] + piece
    branch = jnp.concatenate(parts, axis=1) * jnp.tile(gate, (1, len(parts)))
    arrived(1)
    here = pl.ds(pl.multiple_of(core * length, length), length)
    vis_ref[here, :] = (whole(3) + branch).astype(jnp.bfloat16)

    there = pl.ds(pl.multiple_of((1 - core) * length, length), length)
    half = KVH * HD

    def swap(ref, at, number):
        return pltpu.make_async_remote_copy(
            src_ref=ref.at[at],
            dst_ref=ref.at[at],
            send_sem=swap_sem.at[number],
            recv_sem=swap_sem.at[number + 1],
            device_id={"seq": partner},
            device_id_type=MESH,
        )

    def project(at, first, last):
        vis = vis_ref[at, :]
        for start in range(first, last, 2 * HD):
            cols = slice(start, start + 2 * HD)
            kv_ref[at, cols] = jnp.dot(
                vis, w_ref[:, cols], preferred_element_type=jnp.float32
            ).astype(jnp.bfloat16)

    vis_swap = swap(vis_ref, here, 0)
    key_swap = swap(kv_ref, (here, pl.ds(0, half)), 2)
    vis_swap.start()
    for copy in big:
        copy.wait()
    project(here, 0, half)
    key_swap.start()
    swap(vis_ref, there, 0).wait_recv()
    project(pl.ds(0, keys), half, 2 * half)
    all_of(slots.at[: n - 1], send_sem).wait()
    vis_swap.wait_send()
    key_swap.wait_send()
    swap(kv_ref, (there, pl.ds(0, half)), 2).wait_recv()


def gather_part(n, q, k, v, r, gate, count, seen, w_kv, text):
    images, rows, width = q.shape
    length = n * rows
    keys = images * length
    tokens = seen.shape[0]
    hbm = pl.BlockSpec(memory_space=pltpu.HBM)
    vmem = pl.BlockSpec(memory_space=pltpu.VMEM)
    held = [
        pltpu.with_memory_space_constraint(x, pltpu.HBM)
        for x in (count, seen.reshape(1, tokens), q, k, v, r, w_kv, text)
    ]
    return pl.pallas_call(
        functools.partial(gather_kernel, n, images, rows, width, tokens),
        out_shape=(
            jax.ShapeDtypeStruct((keys, width), jnp.bfloat16),
            jax.ShapeDtypeStruct((2 * keys, tokens), jnp.float32),
            jax.ShapeDtypeStruct((8 * images, keys), jnp.bfloat16),
            jax.ShapeDtypeStruct((keys, w_kv.shape[1]), jnp.bfloat16),
            jax.ShapeDtypeStruct(text.shape, jnp.bfloat16),
        ),
        in_specs=[hbm] * 9,
        out_specs=(vmem,) * 5,
        scratch_shapes=[
            pltpu.VMEM(w_kv.shape, jnp.bfloat16),
            pltpu.VMEM((4, rows, width), jnp.bfloat16),
            pltpu.VMEM((n, 4, rows, width), jnp.bfloat16),
            pltpu.VMEM((1, tokens), jnp.int32),
            pltpu.SMEM((1,), jnp.float32),
            pltpu.SMEM((images,), jnp.int32),
            pltpu.SemaphoreType.DMA,
            pltpu.SemaphoreType.DMA((3,)),
            pltpu.SemaphoreType.DMA((2,)),
            pltpu.SemaphoreType.DMA,
            pltpu.SemaphoreType.DMA((2,)),
            pltpu.SemaphoreType.DMA((4,)),
        ],
        compiler_params=pltpu.CompilerParams(
            collective_id=0, has_side_effects=True, vmem_limit_bytes=GRANT
        ),
        name="vision",
    )(gate, *held)


def text_kernel(
    vis_ref, bias_ref, pick_ref, kv_ref, q_ref,
    vis_out, out_hbm,
    local_ref, o_ref, local_sem, out_sem,
):
    images, rows, width = local_ref.shape
    keys = vis_ref.shape[0]
    half = KVH * HD
    scale = math.log2(math.e) / math.sqrt(HD)
    span = QGROUP * HD

    def double(x):
        zero = jnp.zeros_like(x)
        return jnp.concatenate(
            [jnp.concatenate([x, zero], axis=1), jnp.concatenate([zero, x], axis=1)], axis=0
        )

    def attend(g, k_two, v_two):
        pairs = QGROUP // 2
        wide = 2 * HD
        scores = [
            lax.dot_general(
                k_two, q_ref[:, g * span + j * wide : g * span + (j + 1) * wide],
                (((1,), (1,)), ((), ())), preferred_element_type=jnp.float32,
            )
            for j in range(pairs)
        ]
        bias = bias_ref[:keys, :]
        probs = []
        for score in scores:
            halves = []
            for part in (score[:keys], score[keys:]):
                part = part + bias
                expd = jnp.exp2((part - jnp.max(part, axis=0, keepdims=True)) * scale)
                halves.append(expd * (1.0 / jnp.sum(expd, axis=0, keepdims=True)))
            probs.append(jnp.concatenate(halves, axis=0).astype(jnp.bfloat16))
        parts = [probs] if g < KVH - 1 else [[prob] for prob in probs]
        j = 0
        for part in parts:
            out = lax.dot_general(
                jnp.concatenate(part, axis=1), v_two, (((0,), (0,)), ((), ())),
                preferred_element_type=jnp.float32,
            ).astype(jnp.bfloat16)
            tokens = out.shape[0] // len(part)
            for i in range(len(part)):
                at = g * span + j * wide
                o_ref[:, at : at + wide] = out[i * tokens : (i + 1) * tokens]
                j += 1
            cols = pl.ds(g * span + (j - len(part)) * wide, len(part) * wide)
            pltpu.make_async_copy(o_ref.at[:, cols], out_hbm.at[:, cols], out_sem).start()

    for g in range(KVH):
        attend(
            g,
            double(kv_ref[:, g * HD : (g + 1) * HD]),
            double(kv_ref[:, half + g * HD : half + (g + 1) * HD]),
        )
    local = jnp.dot(pick_ref[...], vis_ref[...], preferred_element_type=jnp.float32)
    for b in range(images):
        local_ref[b] = local[8 * b : 8 * b + rows].astype(jnp.bfloat16)
    local_copy = pltpu.make_async_copy(local_ref, vis_out, local_sem)
    local_copy.start()
    local_copy.wait()
    pltpu.make_async_copy(o_ref, out_hbm, out_sem).wait()


def text_part(shape, vis, bias, pick, kv, query):
    vmem = pl.BlockSpec(memory_space=pltpu.VMEM)
    anyspace = pl.BlockSpec(memory_space=pl.ANY)
    return pl.pallas_call(
        text_kernel,
        out_shape=(
            jax.ShapeDtypeStruct(shape, jnp.bfloat16),
            jax.ShapeDtypeStruct(query.shape, jnp.bfloat16),
        ),
        in_specs=[vmem] * 5,
        out_specs=(anyspace, anyspace),
        scratch_shapes=[
            pltpu.VMEM(shape, jnp.bfloat16),
            pltpu.VMEM(query.shape, jnp.bfloat16),
            pltpu.SemaphoreType.DMA,
            pltpu.SemaphoreType.DMA,
        ],
        compiler_params=pltpu.CompilerParams(vmem_limit_bytes=GRANT),
        name="text",
    )(vis, bias, pick, kv, query)


def fits(n, images, rows, width):
    length = n * rows
    return (
        n == 4 * CORES
        and images == CORES
        and 2 * images * length == LANES
        and LANES % length == 0
        and (width // VHEAD) % (LANES // length) == 0
        and rows <= 8
        and length % 16 == 0
    )


def on_device(n, *args):
    vis_query, vis_key, vis_value, vis_resid, attn_gate, tile_count, w_kv, text_query, text_image = args
    images, rows, width = vis_query.shape
    if not fits(n, images, rows, width):
        return general_form(*args)
    held = gather_part(
        n, vis_query, vis_key, vis_value, vis_resid, attn_gate, tile_count, text_image,
        w_kv, text_query,
    )
    return text_part(vis_query.shape, *held)


def solution(mesh):
    placed = (
        P("group", "seq", None),
        P("group", "seq", None),
        P("group", "seq", None),
        P("group", "seq", None),
        P(),
        P("group"),
        P(),
        P(("group", "seq"), None),
        P(("group", "seq")),
    )
    return jax.shard_map(
        functools.partial(on_device, mesh.shape["seq"]),
        mesh=mesh,
        in_specs=placed,
        out_specs=(P("group", "seq", None), P(("group", "seq"), None)),
        check_vma=False,
    )
```

```python
import functools
import math

import jax
import jax.numpy as jnp
from jax import lax
from jax.experimental import pallas as pl
from jax.experimental.pallas import tpu as pltpu
from jax.sharding import PartitionSpec as P

VHEADS = 16
VHEAD = 80
KVH = 8
HD = 128
QGROUP = 6
TILES = 4
LANES = 128
NEG = -1e30


def vision_attend(query, keys, values, tile_count, nheads):
    images, rows, width = query.shape
    length = keys.shape[1]
    patch = length // TILES
    tile_of = jnp.arange(length, dtype=jnp.int32) // patch
    key_ok = tile_of[None, :] < tile_count[:, None]
    query = query.reshape(images, rows, nheads, VHEAD)
    keys = keys.reshape(images, length, nheads, VHEAD)
    values = values.reshape(images, length, nheads, VHEAD)
    scores = jnp.einsum(
        "bqhd,bkhd->bhqk", query, keys, preferred_element_type=jnp.float32
    ) / math.sqrt(VHEAD)
    scores = jnp.where(key_ok[:, None, None, :], scores, NEG)
    peak = jnp.max(scores, axis=-1, keepdims=True)
    expo = jnp.exp(scores - peak)
    probs = (expo / jnp.sum(expo, axis=-1, keepdims=True)).astype(jnp.bfloat16)
    attn = jnp.einsum("bhqk,bkhd->bqhd", probs, values, preferred_element_type=jnp.float32)
    return attn.reshape(images, rows, width)


def general_form(
    vis_query, vis_key, vis_value, vis_resid, attn_gate, tile_count, w_kv, text_query, text_image
):
    images, rows, width = vis_query.shape
    keys, values = (
        lax.all_gather(vis_key, "seq", axis=1, tiled=True),
        lax.all_gather(vis_value, "seq", axis=1, tiled=True),
    )
    attn = vision_attend(vis_query, keys, values, tile_count, VHEADS)
    vision_out = (vis_resid.astype(jnp.float32) + jnp.tanh(attn_gate[0]) * attn).astype(
        jnp.bfloat16
    )
    local_kv = jnp.dot(
        vision_out.reshape(images * rows, width), w_kv, preferred_element_type=jnp.float32
    )
    local_kv = local_kv.astype(jnp.bfloat16).reshape(images, rows, w_kv.shape[1])
    cross_kv = lax.all_gather(local_kv, "seq", axis=1, tiled=True)
    length = cross_kv.shape[1]
    patch = length // TILES
    tile_of = jnp.arange(length, dtype=jnp.int32) // patch
    key_ok = tile_of[None, :] < tile_count[:, None]
    half = KVH * HD
    flat_kv = cross_kv.reshape(images * length, 2 * half)
    cross_key = flat_kv[:, :half].reshape(images * length, KVH, HD)
    cross_value = flat_kv[:, half:].reshape(images * length, KVH, HD)
    image_of_key = jnp.arange(images * length, dtype=jnp.int32) // length
    flat_ok = key_ok.reshape(images * length)
    tokens = text_query.shape[0]
    qrows = text_query.reshape(tokens, KVH, QGROUP, HD)
    score = jnp.einsum(
        "tgqd,kgd->tgqk", qrows, cross_key, preferred_element_type=jnp.float32
    ) / math.sqrt(HD)
    allowed = (image_of_key[None, :] <= text_image[:, None]) & flat_ok[None, :]
    score = jnp.where(allowed[:, None, None, :], score, NEG)
    top = jnp.max(score, axis=-1, keepdims=True)
    expd = jnp.exp(score - top)
    prob = (expd / jnp.sum(expd, axis=-1, keepdims=True)).astype(jnp.bfloat16)
    out = jnp.einsum("tgqk,kgd->tgqd", prob, cross_value, preferred_element_type=jnp.float32)
    cross_out = out.reshape(tokens, KVH * QGROUP * HD).astype(jnp.bfloat16)
    return (vision_out, cross_out)


GRANT = 16 * 1024 * 1024
MESH = pl.DeviceIdType.MESH
CORES = 2


def gather_kernel(
    n, images, rows, width, tokens,
    gate_in, count_in, seen_in, q_in, k_in, v_in, r_in, w_in, text_in,
    vis_ref, bias_ref, pick_ref, kv_ref, text_ref,
    w_ref, other, slots, seen_ref, gate_ref, count_ref,
    load_sem, small_sem, send_sem, recv_sem, swap_sem,
):
    me = lax.axis_index("seq")
    chip, core = me // CORES, me % CORES
    row, col = chip // 2, chip % 2
    partner = chip * CORES + (1 - core)
    across = row * 2 + (1 - col)
    along = (1 - row) * 2 + col
    corner = (1 - row) * 2 + (1 - col)
    length = n * rows
    keys = images * length

    sources = (q_in, k_in, v_in, r_in)
    mine = slots.at[me]
    loads = [
        pltpu.make_async_copy(ref.at[image], into.at[a], load_sem)
        for a, ref in enumerate(sources)
        for image, into in ((core, mine), (1 - core, other))
    ]

    def all_of(ref, sem):
        return pltpu.make_async_copy(ref, ref, sem)

    barrier = pltpu.get_barrier_semaphore()
    chips = (corner, across, along)
    others = [there * CORES + b for there in chips for b in range(CORES)] + [partner]
    for dev in others:
        pl.semaphore_signal(barrier, inc=1, device_id={"seq": dev}, device_id_type=MESH)
    for load in loads:
        load.start()
    small = [
        pltpu.make_async_copy(gate_in, gate_ref, small_sem.at[0]),
        pltpu.make_async_copy(count_in, count_ref, small_sem.at[1]),
        pltpu.make_async_copy(seen_in, seen_ref, small_sem.at[2]),
    ]
    big = [
        pltpu.make_async_copy(w_in, w_ref, small_sem.at[1]),
        pltpu.make_async_copy(text_in, text_ref, small_sem.at[2]),
    ]
    for copy in small:
        copy.start()
    pl.semaphore_wait(barrier, len(others))
    all_of(slots.at[:2], load_sem).wait()

    cuts = (pl.ds(0, 3), pl.ds(3, 1))

    def send(src, part, dev):
        pltpu.make_async_remote_copy(
            src_ref=src.at[cuts[part]],
            dst_ref=slots.at[me, cuts[part]],
            send_sem=send_sem,
            recv_sem=recv_sem.at[part],
            device_id={"seq": dev},
            device_id_type=MESH,
        ).start()

    for part in range(2):
        for there in chips:
            send(mine, part, there * CORES + core)
            send(other, part, there * CORES + 1 - core)
        send(other, part, partner)
    for copy in small:
        copy.wait()
    for copy in big:
        copy.start()

    place = lax.broadcasted_iota(jnp.int32, (length, tokens), 0)
    for b in range(images):
        ok = (place // (length // TILES) < count_ref[b]) & (seen_ref[...] >= b)
        bias = jnp.where(ok, 0.0, NEG)
        for twin in range(2):
            at = twin * keys + b * length
            bias_ref[at : at + length, :] = bias
    line = lax.broadcasted_iota(jnp.int32, pick_ref.shape, 0)
    want = (line // 8) * length + me * rows + line % 8
    key_at = lax.broadcasted_iota(jnp.int32, pick_ref.shape, 1)
    pick_ref[...] = jnp.where(key_at == want, 1.0, 0.0).astype(jnp.bfloat16)
    gate = jnp.tanh(jnp.full((1, LANES), gate_ref[0], jnp.float32))

    def arrived(part):
        all_of(slots.at[: n - 1, cuts[part]], recv_sem.at[part]).wait()

    def whole(a):
        return jnp.concatenate(
            [slots[s, a].astype(jnp.float32) for s in range(n)], axis=0
        )

    arrived(0)
    query, key, value = (whole(a).astype(jnp.bfloat16) for a in range(3))
    heads = width // VHEAD
    side = LANES // length
    groups = range(0, heads, side)
    key_row = lax.broadcasted_iota(jnp.int32, (length, LANES), 0)
    scale = math.log2(math.e) / math.sqrt(VHEAD)
    count = jnp.where(core == 0, count_ref[0], count_ref[1])
    bias = jnp.where(key_row // (length // TILES) < count, 0.0, NEG)
    windows, owners, scores = [], [], []
    for h in groups:
        lo, hi = h * VHEAD // LANES * LANES, -(-(h + side) * VHEAD // LANES) * LANES
        lane = lax.broadcasted_iota(jnp.int32, (length, hi - lo), 1) + lo
        masks = [(lane >= i * VHEAD) & (lane < (i + 1) * VHEAD) for i in range(h, h + side)]
        window = query[:, lo:hi]
        spread = jnp.concatenate(
            [jnp.where(mask, window, jnp.zeros_like(window)) for mask in masks], axis=0
        )
        score = lax.dot_general(
            key[:, lo:hi], spread, (((1,), (1,)), ((), ())),
            preferred_element_type=jnp.float32,
        )
        windows.append((lo, hi))
        owners.append(masks)
        scores.append(score + bias)
    probs = []
    for score in scores:
        expo = jnp.exp2((score - jnp.max(score, axis=0, keepdims=True)) * scale)
        prob = expo * (1.0 / jnp.sum(expo, axis=0, keepdims=True))
        probs.append(prob.astype(jnp.bfloat16))
    parts = [None] * (width // LANES)
    for (lo, hi), masks, prob in zip(windows, owners, probs):
        attn = lax.dot_general(
            prob, value[:, lo:hi], (((0,), (0,)), ((), ())),
            preferred_element_type=jnp.float32,
        )
        total = jnp.zeros((length, hi - lo), jnp.float32)
        for i, mask in enumerate(masks):
            total = jnp.where(mask, attn[i * length : (i + 1) * length], total)
        for t in range(lo // LANES, hi // LANES):
            piece = total[:, t * LANES - lo : (t + 1) * LANES - lo]
            parts[t] = piece if parts[t] is None else parts[t] + piece
    branch = jnp.concatenate(parts, axis=1) * jnp.tile(gate, (1, len(parts)))
    arrived(1)
    here = pl.ds(pl.multiple_of(core * length, length), length)
    vis_ref[here, :] = (whole(3) + branch).astype(jnp.bfloat16)

    there = pl.ds(pl.multiple_of((1 - core) * length, length), length)
    half = KVH * HD

    def swap(ref, at, sent, number):
        return pltpu.make_async_remote_copy(
            src_ref=ref.at[at],
            dst_ref=ref.at[at],
            send_sem=sent,
            recv_sem=swap_sem.at[number],
            device_id={"seq": partner},
            device_id_type=MESH,
        )

    def project(at, first, last):
        vis = vis_ref[at, :]
        for start in range(first, last, 2 * HD):
            cols = slice(start, start + 2 * HD)
            kv_ref[at, cols] = jnp.dot(
                vis, w_ref[:, cols], preferred_element_type=jnp.float32
            ).astype(jnp.bfloat16)

    vis_swap = swap(vis_ref, here, load_sem, 0)
    key_swap = swap(kv_ref, (here, pl.ds(0, half)), small_sem.at[0], 1)
    vis_swap.start()
    for copy in big:
        copy.wait()
    project(here, 0, half)
    key_swap.start()
    swap(vis_ref, there, load_sem, 0).wait_recv()
    project(pl.ds(0, keys), half, 2 * half)
    all_of(slots.at[: n - 1], send_sem).wait()
    vis_swap.wait_send()
    key_swap.wait_send()
    swap(kv_ref, (there, pl.ds(0, half)), small_sem.at[0], 1).wait_recv()


def gather_part(n, q, k, v, r, gate, count, seen, w_kv, text):
    images, rows, width = q.shape
    length = n * rows
    keys = images * length
    tokens = seen.shape[0]
    hbm = pl.BlockSpec(memory_space=pltpu.HBM)
    vmem = pl.BlockSpec(memory_space=pltpu.VMEM)
    held = [
        pltpu.with_memory_space_constraint(x, pltpu.HBM)
        for x in (count, seen.reshape(1, tokens), q, k, v, r, w_kv, text)
    ]
    return pl.pallas_call(
        functools.partial(gather_kernel, n, images, rows, width, tokens),
        out_shape=(
            jax.ShapeDtypeStruct((keys, width), jnp.bfloat16),
            jax.ShapeDtypeStruct((2 * keys, tokens), jnp.float32),
            jax.ShapeDtypeStruct((8 * images, keys), jnp.bfloat16),
            jax.ShapeDtypeStruct((keys, w_kv.shape[1]), jnp.bfloat16),
            jax.ShapeDtypeStruct(text.shape, jnp.bfloat16),
        ),
        in_specs=[hbm] * 9,
        out_specs=(vmem,) * 5,
        scratch_shapes=[
            pltpu.VMEM(w_kv.shape, jnp.bfloat16),
            pltpu.VMEM((4, rows, width), jnp.bfloat16),
            pltpu.VMEM((n, 4, rows, width), jnp.bfloat16),
            pltpu.VMEM((1, tokens), jnp.int32),
            pltpu.SMEM((1,), jnp.float32),
            pltpu.SMEM((images,), jnp.int32),
            pltpu.SemaphoreType.DMA,
            pltpu.SemaphoreType.DMA((3,)),
            pltpu.SemaphoreType.DMA,
            pltpu.SemaphoreType.DMA((2,)),
            pltpu.SemaphoreType.DMA((2,)),
        ],
        compiler_params=pltpu.CompilerParams(
            collective_id=0, has_side_effects=True, vmem_limit_bytes=GRANT
        ),
        name="vision",
    )(gate, *held)


def text_kernel(
    vis_ref, bias_ref, pick_ref, kv_ref, q_ref,
    vis_out, out_hbm,
    local_ref, o_ref, local_sem, out_sem,
):
    images, rows, width = local_ref.shape
    keys = vis_ref.shape[0]
    half = KVH * HD
    scale = math.log2(math.e) / math.sqrt(HD)
    span = QGROUP * HD

    def double(x):
        zero = jnp.zeros_like(x)
        return jnp.concatenate(
            [jnp.concatenate([x, zero], axis=1), jnp.concatenate([zero, x], axis=1)], axis=0
        )

    def attend(g, k_two, v_two):
        pairs = QGROUP // 2
        wide = 2 * HD
        scores = [
            lax.dot_general(
                k_two, q_ref[:, g * span + j * wide : g * span + (j + 1) * wide],
                (((1,), (1,)), ((), ())), preferred_element_type=jnp.float32,
            )
            for j in range(pairs)
        ]
        bias = bias_ref[:keys, :]
        probs = []
        for score in scores:
            halves = []
            for part in (score[:keys], score[keys:]):
                part = part + bias
                expd = jnp.exp2((part - jnp.max(part, axis=0, keepdims=True)) * scale)
                halves.append(expd * (1.0 / jnp.sum(expd, axis=0, keepdims=True)))
            probs.append(jnp.concatenate(halves, axis=0).astype(jnp.bfloat16))
        parts = [probs] if g < KVH - 1 else [[prob] for prob in probs]
        j = 0
        for part in parts:
            out = lax.dot_general(
                jnp.concatenate(part, axis=1), v_two, (((0,), (0,)), ((), ())),
                preferred_element_type=jnp.float32,
            ).astype(jnp.bfloat16)
            tokens = out.shape[0] // len(part)
            for i in range(len(part)):
                at = g * span + j * wide
                o_ref[:, at : at + wide] = out[i * tokens : (i + 1) * tokens]
                j += 1
            cols = pl.ds(g * span + (j - len(part)) * wide, len(part) * wide)
            pltpu.make_async_copy(o_ref.at[:, cols], out_hbm.at[:, cols], out_sem).start()

    for g in range(KVH):
        attend(
            g,
            double(kv_ref[:, g * HD : (g + 1) * HD]),
            double(kv_ref[:, half + g * HD : half + (g + 1) * HD]),
        )
    local = jnp.dot(pick_ref[...], vis_ref[...], preferred_element_type=jnp.float32)
    for b in range(images):
        local_ref[b] = local[8 * b : 8 * b + rows].astype(jnp.bfloat16)
    local_copy = pltpu.make_async_copy(local_ref, vis_out, local_sem)
    local_copy.start()
    local_copy.wait()
    pltpu.make_async_copy(o_ref, out_hbm, out_sem).wait()


def text_part(shape, vis, bias, pick, kv, query):
    vmem = pl.BlockSpec(memory_space=pltpu.VMEM)
    anyspace = pl.BlockSpec(memory_space=pl.ANY)
    return pl.pallas_call(
        text_kernel,
        out_shape=(
            jax.ShapeDtypeStruct(shape, jnp.bfloat16),
            jax.ShapeDtypeStruct(query.shape, jnp.bfloat16),
        ),
        in_specs=[vmem] * 5,
        out_specs=(anyspace, anyspace),
        scratch_shapes=[
            pltpu.VMEM(shape, jnp.bfloat16),
            pltpu.VMEM(query.shape, jnp.bfloat16),
            pltpu.SemaphoreType.DMA,
            pltpu.SemaphoreType.DMA,
        ],
        compiler_params=pltpu.CompilerParams(vmem_limit_bytes=GRANT),
        name="text",
    )(vis, bias, pick, kv, query)


def fits(n, images, rows, width):
    length = n * rows
    return (
        n == 4 * CORES
        and images == CORES
        and 2 * images * length == LANES
        and LANES % length == 0
        and (width // VHEAD) % (LANES // length) == 0
        and rows <= 8
        and length % 16 == 0
    )


def on_device(n, *args):
    vis_query, vis_key, vis_value, vis_resid, attn_gate, tile_count, w_kv, text_query, text_image = args
    images, rows, width = vis_query.shape
    if not fits(n, images, rows, width):
        return general_form(*args)
    held = gather_part(
        n, vis_query, vis_key, vis_value, vis_resid, attn_gate, tile_count, text_image,
        w_kv, text_query,
    )
    return text_part(vis_query.shape, *held)


def solution(mesh):
    placed = (
        P("group", "seq", None),
        P("group", "seq", None),
        P("group", "seq", None),
        P("group", "seq", None),
        P(),
        P("group"),
        P(),
        P(("group", "seq"), None),
        P(("group", "seq")),
    )
    return jax.shard_map(
        functools.partial(on_device, mesh.shape["seq"]),
        mesh=mesh,
        in_specs=placed,
        out_specs=(P("group", "seq", None), P(("group", "seq"), None)),
        check_vma=False,
    )
```

```python
import functools
import math

import jax
import jax.numpy as jnp
from jax import lax
from jax.experimental import pallas as pl
from jax.experimental.pallas import tpu as pltpu
from jax.sharding import PartitionSpec as P

VHEADS = 16
VHEAD = 80
KVH = 8
HD = 128
QGROUP = 6
TILES = 4
LANES = 128
NEG = -1e30


def vision_attend(query, keys, values, tile_count, nheads):
    images, rows, width = query.shape
    length = keys.shape[1]
    patch = length // TILES
    tile_of = jnp.arange(length, dtype=jnp.int32) // patch
    key_ok = tile_of[None, :] < tile_count[:, None]
    query = query.reshape(images, rows, nheads, VHEAD)
    keys = keys.reshape(images, length, nheads, VHEAD)
    values = values.reshape(images, length, nheads, VHEAD)
    scores = jnp.einsum(
        "bqhd,bkhd->bhqk", query, keys, preferred_element_type=jnp.float32
    ) / math.sqrt(VHEAD)
    scores = jnp.where(key_ok[:, None, None, :], scores, NEG)
    peak = jnp.max(scores, axis=-1, keepdims=True)
    expo = jnp.exp(scores - peak)
    probs = (expo / jnp.sum(expo, axis=-1, keepdims=True)).astype(jnp.bfloat16)
    attn = jnp.einsum("bhqk,bkhd->bqhd", probs, values, preferred_element_type=jnp.float32)
    return attn.reshape(images, rows, width)


def general_form(
    vis_query, vis_key, vis_value, vis_resid, attn_gate, tile_count, w_kv, text_query, text_image
):
    images, rows, width = vis_query.shape
    keys, values = (
        lax.all_gather(vis_key, "seq", axis=1, tiled=True),
        lax.all_gather(vis_value, "seq", axis=1, tiled=True),
    )
    attn = vision_attend(vis_query, keys, values, tile_count, VHEADS)
    vision_out = (vis_resid.astype(jnp.float32) + jnp.tanh(attn_gate[0]) * attn).astype(
        jnp.bfloat16
    )
    local_kv = jnp.dot(
        vision_out.reshape(images * rows, width), w_kv, preferred_element_type=jnp.float32
    )
    local_kv = local_kv.astype(jnp.bfloat16).reshape(images, rows, w_kv.shape[1])
    cross_kv = lax.all_gather(local_kv, "seq", axis=1, tiled=True)
    length = cross_kv.shape[1]
    patch = length // TILES
    tile_of = jnp.arange(length, dtype=jnp.int32) // patch
    key_ok = tile_of[None, :] < tile_count[:, None]
    half = KVH * HD
    flat_kv = cross_kv.reshape(images * length, 2 * half)
    cross_key = flat_kv[:, :half].reshape(images * length, KVH, HD)
    cross_value = flat_kv[:, half:].reshape(images * length, KVH, HD)
    image_of_key = jnp.arange(images * length, dtype=jnp.int32) // length
    flat_ok = key_ok.reshape(images * length)
    tokens = text_query.shape[0]
    qrows = text_query.reshape(tokens, KVH, QGROUP, HD)
    score = jnp.einsum(
        "tgqd,kgd->tgqk", qrows, cross_key, preferred_element_type=jnp.float32
    ) / math.sqrt(HD)
    allowed = (image_of_key[None, :] <= text_image[:, None]) & flat_ok[None, :]
    score = jnp.where(allowed[:, None, None, :], score, NEG)
    top = jnp.max(score, axis=-1, keepdims=True)
    expd = jnp.exp(score - top)
    prob = (expd / jnp.sum(expd, axis=-1, keepdims=True)).astype(jnp.bfloat16)
    out = jnp.einsum("tgqk,kgd->tgqd", prob, cross_value, preferred_element_type=jnp.float32)
    cross_out = out.reshape(tokens, KVH * QGROUP * HD).astype(jnp.bfloat16)
    return (vision_out, cross_out)


GRANT = 16 * 1024 * 1024
MESH = pl.DeviceIdType.MESH
CORES = 2


def gather_kernel(
    n, images, rows, width, tokens,
    gate_in, count_in, seen_in, q_in, k_in, v_in, r_in, w_in, text_in,
    vis_ref, bias_ref, pick_ref, kv_ref, text_ref,
    w_ref, other, slots, seen_ref, gate_ref, count_ref,
    load_sem, small_sem, recv_sem, swap_sem,
):
    me = lax.axis_index("seq")
    chip, core = me // CORES, me % CORES
    row, col = chip // 2, chip % 2
    partner = chip * CORES + (1 - core)
    across = row * 2 + (1 - col)
    along = (1 - row) * 2 + col
    corner = (1 - row) * 2 + (1 - col)
    length = n * rows
    keys = images * length

    sources = (q_in, k_in, v_in, r_in)
    mine = slots.at[me]
    loads = [
        pltpu.make_async_copy(ref.at[image], into.at[a], load_sem)
        for a, ref in enumerate(sources)
        for image, into in ((core, mine), (1 - core, other))
    ]

    def all_of(ref, sem):
        return pltpu.make_async_copy(ref, ref, sem)

    barrier = pltpu.get_barrier_semaphore()
    chips = (corner, across, along)
    others = [there * CORES + b for there in chips for b in range(CORES)] + [partner]
    for dev in others:
        pl.semaphore_signal(barrier, inc=1, device_id={"seq": dev}, device_id_type=MESH)
    for load in loads:
        load.start()
    small = [
        pltpu.make_async_copy(gate_in, gate_ref, small_sem.at[0]),
        pltpu.make_async_copy(count_in, count_ref, small_sem.at[1]),
        pltpu.make_async_copy(seen_in, seen_ref, small_sem.at[2]),
    ]
    big = [
        pltpu.make_async_copy(w_in, w_ref, small_sem.at[1]),
        pltpu.make_async_copy(text_in, text_ref, small_sem.at[2]),
    ]
    for copy in small:
        copy.start()
    pl.semaphore_wait(barrier, len(others))
    all_of(slots.at[:2], load_sem).wait()
    for copy in small:
        copy.wait()

    cuts = (pl.ds(0, 3), pl.ds(3, 1))

    def send(src, part, dev):
        pltpu.make_async_remote_copy(
            src_ref=src.at[cuts[part]],
            dst_ref=slots.at[me, cuts[part]],
            send_sem=small_sem.at[0],
            recv_sem=recv_sem.at[part],
            device_id={"seq": dev},
            device_id_type=MESH,
        ).start()

    for part in range(2):
        for there in chips:
            send(mine, part, there * CORES + core)
            send(other, part, there * CORES + 1 - core)
        send(other, part, partner)
    for copy in big:
        copy.start()

    place = lax.broadcasted_iota(jnp.int32, (length, tokens), 0)
    for b in range(images):
        ok = (place // (length // TILES) < count_ref[b]) & (seen_ref[...] >= b)
        bias = jnp.where(ok, 0.0, NEG)
        for twin in range(2):
            at = twin * keys + b * length
            bias_ref[at : at + length, :] = bias
    line = lax.broadcasted_iota(jnp.int32, pick_ref.shape, 0)
    want = (line // 8) * length + me * rows + line % 8
    key_at = lax.broadcasted_iota(jnp.int32, pick_ref.shape, 1)
    pick_ref[...] = jnp.where(key_at == want, 1.0, 0.0).astype(jnp.bfloat16)
    gate = jnp.tanh(jnp.full((1, LANES), gate_ref[0], jnp.float32))

    def arrived(part):
        all_of(slots.at[: n - 1, cuts[part]], recv_sem.at[part]).wait()

    def whole(a):
        return jnp.concatenate(
            [slots[s, a].astype(jnp.float32) for s in range(n)], axis=0
        )

    arrived(0)
    query, key, value = (whole(a).astype(jnp.bfloat16) for a in range(3))
    heads = width // VHEAD
    side = LANES // length
    groups = range(0, heads, side)
    key_row = lax.broadcasted_iota(jnp.int32, (length, LANES), 0)
    scale = math.log2(math.e) / math.sqrt(VHEAD)
    count = jnp.where(core == 0, count_ref[0], count_ref[1])
    bias = jnp.where(key_row // (length // TILES) < count, 0.0, NEG)
    windows, owners, scores = [], [], []
    for h in groups:
        lo, hi = h * VHEAD // LANES * LANES, -(-(h + side) * VHEAD // LANES) * LANES
        lane = lax.broadcasted_iota(jnp.int32, (length, hi - lo), 1) + lo
        masks = [(lane >= i * VHEAD) & (lane < (i + 1) * VHEAD) for i in range(h, h + side)]
        window = query[:, lo:hi]
        spread = jnp.concatenate(
            [jnp.where(mask, window, jnp.zeros_like(window)) for mask in masks], axis=0
        )
        score = lax.dot_general(
            key[:, lo:hi], spread, (((1,), (1,)), ((), ())),
            preferred_element_type=jnp.float32,
        )
        windows.append((lo, hi))
        owners.append(masks)
        scores.append(score + bias)
    probs = []
    for score in scores:
        expo = jnp.exp2((score - jnp.max(score, axis=0, keepdims=True)) * scale)
        prob = expo * (1.0 / jnp.sum(expo, axis=0, keepdims=True))
        probs.append(prob.astype(jnp.bfloat16))
    parts = [None] * (width // LANES)
    for (lo, hi), masks, prob in zip(windows, owners, probs):
        attn = lax.dot_general(
            prob, value[:, lo:hi], (((0,), (0,)), ((), ())),
            preferred_element_type=jnp.float32,
        )
        total = jnp.zeros((length, hi - lo), jnp.float32)
        for i, mask in enumerate(masks):
            total = jnp.where(mask, attn[i * length : (i + 1) * length], total)
        for t in range(lo // LANES, hi // LANES):
            piece = total[:, t * LANES - lo : (t + 1) * LANES - lo]
            parts[t] = piece if parts[t] is None else parts[t] + piece
    branch = jnp.concatenate(parts, axis=1) * jnp.tile(gate, (1, len(parts)))
    arrived(1)
    here = pl.ds(pl.multiple_of(core * length, length), length)
    vis_ref[here, :] = (whole(3) + branch).astype(jnp.bfloat16)

    there = pl.ds(pl.multiple_of((1 - core) * length, length), length)
    half = KVH * HD

    def swap(ref, at, sent, number):
        return pltpu.make_async_remote_copy(
            src_ref=ref.at[at],
            dst_ref=ref.at[at],
            send_sem=sent,
            recv_sem=swap_sem.at[number],
            device_id={"seq": partner},
            device_id_type=MESH,
        )

    def project(at, first, last):
        vis = vis_ref[at, :]
        for start in range(first, last, 2 * HD):
            cols = slice(start, start + 2 * HD)
            kv_ref[at, cols] = jnp.dot(
                vis, w_ref[:, cols], preferred_element_type=jnp.float32
            ).astype(jnp.bfloat16)

    vis_swap = swap(vis_ref, here, load_sem, 0)
    key_swap = swap(kv_ref, (here, pl.ds(0, half)), small_sem.at[1], 1)
    vis_swap.start()
    for copy in big:
        copy.wait()
    project(here, 0, half)
    key_swap.start()
    swap(vis_ref, there, load_sem, 0).wait_recv()
    project(pl.ds(0, keys), half, 2 * half)
    all_of(slots.at[: n - 1], small_sem.at[0]).wait()
    vis_swap.wait_send()
    key_swap.wait_send()
    swap(kv_ref, (there, pl.ds(0, half)), small_sem.at[1], 1).wait_recv()


def gather_part(n, q, k, v, r, gate, count, seen, w_kv, text):
    images, rows, width = q.shape
    length = n * rows
    keys = images * length
    tokens = seen.shape[0]
    hbm = pl.BlockSpec(memory_space=pltpu.HBM)
    vmem = pl.BlockSpec(memory_space=pltpu.VMEM)
    held = [
        pltpu.with_memory_space_constraint(x, pltpu.HBM)
        for x in (count, seen.reshape(1, tokens), q, k, v, r, w_kv, text)
    ]
    return pl.pallas_call(
        functools.partial(gather_kernel, n, images, rows, width, tokens),
        out_shape=(
            jax.ShapeDtypeStruct((keys, width), jnp.bfloat16),
            jax.ShapeDtypeStruct((2 * keys, tokens), jnp.float32),
            jax.ShapeDtypeStruct((8 * images, keys), jnp.bfloat16),
            jax.ShapeDtypeStruct((keys, w_kv.shape[1]), jnp.bfloat16),
            jax.ShapeDtypeStruct(text.shape, jnp.bfloat16),
        ),
        in_specs=[hbm] * 9,
        out_specs=(vmem,) * 5,
        scratch_shapes=[
            pltpu.VMEM(w_kv.shape, jnp.bfloat16),
            pltpu.VMEM((4, rows, width), jnp.bfloat16),
            pltpu.VMEM((n, 4, rows, width), jnp.bfloat16),
            pltpu.VMEM((1, tokens), jnp.int32),
            pltpu.SMEM((1,), jnp.float32),
            pltpu.SMEM((images,), jnp.int32),
            pltpu.SemaphoreType.DMA,
            pltpu.SemaphoreType.DMA((3,)),
            pltpu.SemaphoreType.DMA((2,)),
            pltpu.SemaphoreType.DMA((2,)),
        ],
        compiler_params=pltpu.CompilerParams(
            collective_id=0, has_side_effects=True, vmem_limit_bytes=GRANT
        ),
        name="vision",
    )(gate, *held)


def text_kernel(
    vis_ref, bias_ref, pick_ref, kv_ref, q_ref,
    vis_out, out_hbm,
    local_ref, o_ref, local_sem, out_sem,
):
    images, rows, width = local_ref.shape
    keys = vis_ref.shape[0]
    half = KVH * HD
    scale = math.log2(math.e) / math.sqrt(HD)
    span = QGROUP * HD

    def double(x):
        zero = jnp.zeros_like(x)
        return jnp.concatenate(
            [jnp.concatenate([x, zero], axis=1), jnp.concatenate([zero, x], axis=1)], axis=0
        )

    def attend(g, k_two, v_two):
        pairs = QGROUP // 2
        wide = 2 * HD
        scores = [
            lax.dot_general(
                k_two, q_ref[:, g * span + j * wide : g * span + (j + 1) * wide],
                (((1,), (1,)), ((), ())), preferred_element_type=jnp.float32,
            )
            for j in range(pairs)
        ]
        bias = bias_ref[:keys, :]
        probs = []
        for score in scores:
            halves = []
            for part in (score[:keys], score[keys:]):
                part = part + bias
                expd = jnp.exp2((part - jnp.max(part, axis=0, keepdims=True)) * scale)
                halves.append(expd * (1.0 / jnp.sum(expd, axis=0, keepdims=True)))
            probs.append(jnp.concatenate(halves, axis=0).astype(jnp.bfloat16))
        parts = [probs] if g < KVH - 1 else [[prob] for prob in probs]
        j = 0
        for part in parts:
            out = lax.dot_general(
                jnp.concatenate(part, axis=1), v_two, (((0,), (0,)), ((), ())),
                preferred_element_type=jnp.float32,
            ).astype(jnp.bfloat16)
            tokens = out.shape[0] // len(part)
            for i in range(len(part)):
                at = g * span + j * wide
                o_ref[:, at : at + wide] = out[i * tokens : (i + 1) * tokens]
                j += 1
            cols = pl.ds(g * span + (j - len(part)) * wide, len(part) * wide)
            pltpu.make_async_copy(o_ref.at[:, cols], out_hbm.at[:, cols], out_sem).start()

    for g in range(KVH):
        attend(
            g,
            double(kv_ref[:, g * HD : (g + 1) * HD]),
            double(kv_ref[:, half + g * HD : half + (g + 1) * HD]),
        )
    local = jnp.dot(pick_ref[...], vis_ref[...], preferred_element_type=jnp.float32)
    for b in range(images):
        local_ref[b] = local[8 * b : 8 * b + rows].astype(jnp.bfloat16)
    local_copy = pltpu.make_async_copy(local_ref, vis_out, local_sem)
    local_copy.start()
    local_copy.wait()
    pltpu.make_async_copy(o_ref, out_hbm, out_sem).wait()


def text_part(shape, vis, bias, pick, kv, query):
    vmem = pl.BlockSpec(memory_space=pltpu.VMEM)
    anyspace = pl.BlockSpec(memory_space=pl.ANY)
    return pl.pallas_call(
        text_kernel,
        out_shape=(
            jax.ShapeDtypeStruct(shape, jnp.bfloat16),
            jax.ShapeDtypeStruct(query.shape, jnp.bfloat16),
        ),
        in_specs=[vmem] * 5,
        out_specs=(anyspace, anyspace),
        scratch_shapes=[
            pltpu.VMEM(shape, jnp.bfloat16),
            pltpu.VMEM(query.shape, jnp.bfloat16),
            pltpu.SemaphoreType.DMA,
            pltpu.SemaphoreType.DMA,
        ],
        compiler_params=pltpu.CompilerParams(vmem_limit_bytes=GRANT),
        name="text",
    )(vis, bias, pick, kv, query)


def fits(n, images, rows, width):
    length = n * rows
    return (
        n == 4 * CORES
        and images == CORES
        and 2 * images * length == LANES
        and LANES % length == 0
        and (width // VHEAD) % (LANES // length) == 0
        and rows <= 8
        and length % 16 == 0
    )


def on_device(n, *args):
    vis_query, vis_key, vis_value, vis_resid, attn_gate, tile_count, w_kv, text_query, text_image = args
    images, rows, width = vis_query.shape
    if not fits(n, images, rows, width):
        return general_form(*args)
    held = gather_part(
        n, vis_query, vis_key, vis_value, vis_resid, attn_gate, tile_count, text_image,
        w_kv, text_query,
    )
    return text_part(vis_query.shape, *held)


def solution(mesh):
    placed = (
        P("group", "seq", None),
        P("group", "seq", None),
        P("group", "seq", None),
        P("group", "seq", None),
        P(),
        P("group"),
        P(),
        P(("group", "seq"), None),
        P(("group", "seq")),
    )
    return jax.shard_map(
        functools.partial(on_device, mesh.shape["seq"]),
        mesh=mesh,
        in_specs=placed,
        out_specs=(P("group", "seq", None), P(("group", "seq"), None)),
        check_vma=False,
    )
```
